256 devices in a mesh: expert: 64 (over z, y, core), tensor: 4 (over x).
Axes of the slice: x: 4, y: 4, z: 8, core: 2. Of those that a mesh axis runs over, the one named last changes fastest.
Arguments:
- context: bfloat16 [8192, 4096], P('expert', 'tensor'), may hold values from -6 to 6
- residual_in: bfloat16 [8192, 4096], P('expert')
- out_weight: bfloat16 [4096, 4096], P('tensor', 'expert'), may hold values from -0.09375 to 0.09375
- norm_gain: bfloat16 [4096], replicated, may hold values from 0.099609375 to 1.8984375
- expert_ids: int32 [8192, 8], P('expert'), may hold values from 0 to 63, all different within a row; in each aligned block of 128 rows (0 to 127, 128 to 255, ...) at most 18 rows name the same one
- gate_weights: float32 [8192, 8], P('expert'), may hold values from 0.1 to 1
- gate_matrix: bfloat16 [64, 4096, 1536], P('expert', None, 'tensor'), may hold values from -0.09375 to 0.09375
- lift_matrix: bfloat16 [64, 4096, 1536], P('expert', None, 'tensor'), may hold values from -0.09375 to 0.09375
- down_matrix: bfloat16 [64, 1536, 4096], P('expert', 'tensor'), may hold values from -0.15625 to 0.15625
Outputs:
- layer_out: bfloat16 [8192, 4096], P('expert', 'tensor')
The draws below stay inside these ranges and needn't reach their ends.
Inputs may be any that keep to these rules, and one draw needn't show every extreme that they name: `expert_ids`: each row names 8 different experts. Within each aligned block of 128 rows (the rows of one index of the expert axis) no expert is named more than 18 times, a bound that some block reaches.
All inputs are finite; a program needn't handle non-finite values.
Results may differ from the reference program's by a relative error of at most 0.009.
Values may be sent and summed in bfloat16 or wider, within the bound.
No kernel may reach another device: no remote copies, remote signals or barrier semaphores. Data moves between devices by JAX's collectives and lax.ppermute only.
A program may use at most 128 MiB of HBM per device.

```python
import math
import jax
import jax.numpy as jnp
import numpy as np
from jax import lax

D = 4096
HEADS = 32
HD = 128
FF = 1536
TOP = 8
TOK_DEV = 128
TOKENS = 8192
EXPERTS = 64
CAP = 18
N_EXPERT = 64
N_TENSOR = 4


def draw_residual_in(key, part):
    noise_key, rough_key, row_key = jax.random.split(key, 3)
    columns = jnp.arange(D).astype(jnp.float32) / D
    rising = 0.5 * jnp.power(3.0, columns)
    roughness = jax.random.uniform(rough_key, (D,), jnp.float32, 0.6, 1.6)
    row_power = jax.random.uniform(row_key, (TOKENS, 1), jnp.float32, -0.5, 0.5)
    base_values = jax.random.normal(noise_key, (TOKENS, D), jnp.float32)
    row_scale = jnp.power(10.0, row_power)
    return (base_values * row_scale * rising[None, :] * roughness[None, :]).astype(jnp.bfloat16)


def steps_of(own_key, extent, cuts, low, high):
    loudness = 1.0
    for axis_at, shards_of in cuts:
        heights = jax.random.uniform(jax.random.fold_in(jax.random.fold_in(own_key, 6), axis_at), (shards_of,), jnp.float32, low / len(cuts), high / len(cuts))
        loudness = loudness * jnp.repeat(jnp.exp(heights), extent[axis_at] // shards_of).reshape((-1,) + (1,) * (len(extent) - 1 - axis_at))
    return loudness


def assign_block(key, own, number, rows, number_of, top, bound, slope):
    ranking = jax.random.permutation(key, number_of)
    packed, common = shares(number_of, rows * top, bound, slope, True), shares(number_of, rows * top, bound, slope, False)
    places = jnp.arange(number_of)

    def named(lengths, rotation):
        used = int((lengths > 0).sum())
        fixed = max(1, used // 4)
        moved = fixed + (places - fixed + rotation * (used - fixed)) % max(1, number_of - fixed)
        return jnp.zeros((number_of,), jnp.int32).at[ranking[jnp.where(places < fixed, places, moved)]].set(jnp.asarray(lengths, jnp.int32))

    lengths = jnp.where(number % 4 == 0, named(packed, number // 4), named(common, number - number // 4 - 1))
    mixed = jax.random.permutation(jax.random.fold_in(own, 3), number_of)
    source_of, receiver = mixed[0:number_of // 2 * 2:2], mixed[1:number_of // 2 * 2:2]
    margin = jnp.minimum(lengths[source_of] - 1, bound - lengths[receiver]) // 2
    margin = jnp.where((source_of == ranking[0]) | (receiver == ranking[0]) | (lengths[receiver] == 0), 0, jnp.maximum(margin, 0))
    moved = jax.random.randint(jax.random.fold_in(own, 4), (number_of // 2,), 0, 1 << 20) % (margin + 1)
    lengths = lengths.at[source_of].add(-moved).at[receiver].add(moved)
    labels = jnp.searchsorted(jnp.cumsum(lengths), jnp.arange(rows * top), side="right").astype(jnp.int32)
    grid = labels.reshape(top, rows).T
    grid = grid[jax.random.permutation(jax.random.fold_in(own, 1), rows)]
    rotation = jax.random.randint(jax.random.fold_in(own, 2), (rows, 1), 0, top)
    return jnp.take_along_axis(grid, (jnp.arange(top)[None, :] + rotation) % top, axis=1)


def shares(amount, total, reach, slope, full):
    weights = [(1 << 20) // math.isqrt(rank ** slope) + 1 for rank in range(1, amount + 1)]
    largest = reach if full else min(reach, max(-(-total // amount), total * weights[0] // sum(weights)))
    least = 1 if total - largest >= amount - 1 else 0
    given, surplus = [largest] + [least] * (amount - 1), total - largest - least * (amount - 1)
    while surplus > 0:
        candidates = [i for i in range(1, amount) if given[i] < largest] or [i for i in range(1, amount) if given[i] < reach]
        pool, left = sum([weights[i] for i in candidates]), surplus
        for i in candidates:
            more = min(reach - given[i], max(1, left * weights[i] // pool), surplus)
            given[i] = given[i] + more
            surplus = surplus - more
    return np.array(given)


def scatter_about(stream_key, shape, scale, reach, pieces=(), held_as=jnp.bfloat16):
    drawn = scale * jax.random.normal(stream_key, shape, jnp.float32)
    if pieces:
        drawn = drawn * steps_of(stream_key, shape, pieces, -0.22, 0.18)
    return jnp.clip(drawn, -reach, reach).astype(held_as)


def setup_inputs(seed: int = 0) -> dict:
    streams_of = jax.random.split(jax.random.key(seed), 10)
    context = scatter_about(streams_of[0], (TOKENS, HEADS * HD), 1.0, 6.0, ((0, 64), (1, 4)))
    residual_in = draw_residual_in(jax.random.fold_in(streams_of[9], 71), 0)
    out_weight = scatter_about(streams_of[2], (HEADS * HD, D), (HEADS * HD) ** -0.5, 0.09375, ((0, 4), (1, 64)))
    norm_gain = jnp.clip(1.0 + 0.18 * jax.random.normal(streams_of[3], (D,), jnp.float32), 0.099609375, 1.8984375).astype(jnp.bfloat16)
    expert_ids_keys = jax.random.split(jax.random.fold_in(streams_of[4], 1), TOKENS // TOK_DEV)
    expert_ids_turns = jax.random.permutation(jax.random.fold_in(streams_of[4], 3), TOKENS // TOK_DEV)
    expert_ids = jax.vmap(lambda own, number: assign_block(jax.random.fold_in(streams_of[4], 2), own, number, TOK_DEV, EXPERTS, TOP, CAP, 2))(expert_ids_keys, expert_ids_turns).reshape((TOKENS, TOP))
    gate_weights = jnp.clip(jnp.exp(math.log(1.0) - 2.3025851 * jax.random.uniform(streams_of[5], (TOKENS, TOP), jnp.float32) ** steps_of(streams_of[5], (TOKENS, TOP), ((0, 64),), -0.2, 0.2)), 0.1, 1.0)
    gate_matrix = scatter_about(streams_of[6], (EXPERTS, D, FF), D ** -0.5, 0.09375, ((0, 64), (2, 4)))
    lift_matrix = scatter_about(streams_of[7], (EXPERTS, D, FF), D ** -0.5, 0.09375, ((0, 64), (2, 4)))
    down_matrix = scatter_about(streams_of[8], (EXPERTS, FF, D), FF ** -0.5, 0.15625, ((0, 64), (1, 4)))
    return dict(context=context, residual_in=residual_in, out_weight=out_weight, norm_gain=norm_gain, expert_ids=expert_ids, gate_weights=gate_weights, gate_matrix=gate_matrix, lift_matrix=lift_matrix, down_matrix=down_matrix)


epsilon = 1e-06

def reference(context, residual_in, out_weight, norm_gain, expert_ids, gate_weights, gate_matrix, lift_matrix, down_matrix):
    attention_out = jnp.dot(context, out_weight, preferred_element_type=jnp.float32)
    hidden_state = (residual_in.astype(jnp.float32) + attention_out).astype(jnp.bfloat16)
    widened = hidden_state.astype(jnp.float32)
    squares_mean = lax.optimization_barrier(jnp.mean(widened * widened, axis=1, keepdims=True))
    normed = (widened * lax.rsqrt(squares_mean + epsilon) * norm_gain.astype(jnp.float32)).astype(jnp.bfloat16)
    flat_ids = expert_ids.reshape(-1)
    flat_gates = gate_weights.reshape(-1)
    rows_max = N_EXPERT * CAP
    block_width = FF // N_TENSOR

    def one_expert(carried, expert):
        matches = flat_ids == expert
        positions = jnp.nonzero(matches, size=rows_max, fill_value=0)[0]
        valid_rows = jnp.arange(rows_max) < jnp.sum(matches)
        token_rows = positions // TOP
        picked_rows = normed[token_rows]
        gate_values = jnp.dot(picked_rows, gate_matrix[expert], preferred_element_type=jnp.float32)
        lift_values = jnp.dot(picked_rows, lift_matrix[expert], preferred_element_type=jnp.float32)
        activation = (jax.nn.silu(gate_values) * lift_values).astype(jnp.bfloat16)
        down_here = down_matrix[expert]
        total_out = jnp.zeros((rows_max, D), jnp.float32)
        for block_index in range(N_TENSOR):
            partial_out = jnp.dot(activation[:, block_index * block_width:(block_index + 1) * block_width], down_here[block_index * block_width:(block_index + 1) * block_width], preferred_element_type=jnp.float32).astype(jnp.bfloat16)
            partial_out = lax.optimization_barrier(partial_out)
            total_out = total_out + partial_out.astype(jnp.float32)
        rounded_out = lax.optimization_barrier(total_out.astype(jnp.bfloat16)).astype(jnp.float32)
        scales = jnp.where(valid_rows, flat_gates[positions], jnp.float32(0.0))
        carried = carried.at[token_rows].add(scales[:, None] * rounded_out)
        return (carried, None)
    moe_sum, _ = lax.scan(one_expert, jnp.zeros((TOKENS, D), jnp.float32), jnp.arange(EXPERTS, dtype=jnp.int32))
    return (widened + moe_sum).astype(jnp.bfloat16)
```

```python
import functools

import jax
import jax.numpy as jnp
from jax import lax
from jax.experimental import pallas as pl
from jax.experimental.pallas import tpu as pltpu
from jax.sharding import Mesh
from jax.sharding import PartitionSpec as P

epsilon = 1e-06
f32 = jnp.float32
bf16 = jnp.bfloat16
NZ, NY, NC, NX = 8, 4, 2, 4
NE = NZ * NY * NC
ND = NY * NC


def whole(*shape):
    return pl.BlockSpec(shape, lambda *_: (0,) * len(shape))


def params(mib):
    return pltpu.CompilerParams(vmem_limit_bytes=mib << 20)


def route_kernel(ids_ref, gates_ref, table_ref):
    tokens = ids_ref.shape[1]
    experts = lax.broadcasted_iota(jnp.int32, (NE, tokens), 0)
    chosen = jnp.zeros((NE, tokens), f32)
    weight = jnp.zeros((NE, tokens), f32)
    for k in range(ids_ref.shape[0]):
        same = experts == ids_ref[k : k + 1, :]
        chosen = jnp.where(same, 1.0, chosen)
        weight = jnp.where(same, gates_ref[k : k + 1, :], weight)
    rows = lax.broadcasted_iota(jnp.int32, (tokens, tokens), 0)
    columns = lax.broadcasted_iota(jnp.int32, (tokens, tokens), 1)
    before = jnp.where(rows < columns, 1.0, 0.0).astype(bf16)
    rank = jnp.dot(chosen.astype(bf16), before, preferred_element_type=f32)
    slot = jnp.where(chosen > 0.0, rank, -1.0)
    table_ref[:, :ND, :] = slot.reshape(NZ, ND, tokens)
    table_ref[:, ND:, :] = weight.reshape(NZ, ND, tokens)


def positions(table_ref, d, capacity):
    parts = []
    for z in range(NZ):
        slot = table_ref[z, d : d + 1, :]
        parts.append(jnp.where(slot >= 0.0, slot + float(z * capacity), -1.0))
    return jnp.concatenate(parts, axis=1).astype(jnp.int32)


def dispatch_kernel(capacity, table_ref, hidden_ref, out_ref):
    hidden = jnp.concatenate([hidden_ref[z] for z in range(NZ)], axis=1)
    tokens = hidden.shape[0]
    slots = lax.broadcasted_iota(jnp.int32, (NZ * capacity, tokens), 0)
    for d in range(ND):
        pick = jnp.where(slots == positions(table_ref, d, capacity), 1.0, 0.0).astype(bf16)
        out_ref[d] = jnp.dot(pick, hidden, preferred_element_type=f32).astype(bf16)


def combine_kernel(capacity, table_ref, rows_ref, out_ref, total_ref):
    tokens = out_ref.shape[0] * out_ref.shape[1]
    slots = lax.broadcasted_iota(jnp.int32, (NZ * capacity, tokens), 0)
    d = pl.program_id(0)
    parts, gates = [], []
    for z in range(NZ):
        slot = table_ref[z, pl.ds(d, 1), :]
        parts.append(jnp.where(slot >= 0.0, slot + float(z * capacity), -1.0))
        gates.append(table_ref[z, pl.ds(ND + d, 1), :])
    place = jnp.concatenate(parts, axis=1).astype(jnp.int32)
    gate = jnp.concatenate(gates, axis=1)
    spread = jnp.where(slots == place, gate, 0.0)
    high = spread.astype(bf16)
    low = (spread - high.astype(f32)).astype(bf16)
    over = (((0,), (0,)), ((), ()))
    got = rows_ref[0]
    part = lax.dot_general(high, got, over, preferred_element_type=f32)
    part = part + lax.dot_general(low, got, over, preferred_element_type=f32)

    @pl.when(d == 0)
    def _():
        total_ref[...] = part

    @pl.when(d > 0)
    def _():
        total_ref[...] += part

    @pl.when(d == pl.num_programs(0) - 1)
    def _():
        out_ref[...] = total_ref[...].astype(out_ref.dtype).reshape(out_ref.shape)


def up_kernel(width, x_ref, gain_ref, gate_ref, lift_ref, out_ref):
    squares = None
    for q in range(NX):
        h = x_ref[q].astype(f32)
        s = jnp.sum(h * h, axis=1, keepdims=True)
        squares = s if squares is None else squares + s
    scale = lax.rsqrt(squares * (1.0 / width) + epsilon)
    gate = lift = None
    for q in range(NX):
        part = x_ref.shape[2]
        normed = (x_ref[q].astype(f32) * scale * gain_ref[q : q + 1, :]).astype(bf16)
        g = jnp.dot(normed, gate_ref[:, q].reshape(part, -1), preferred_element_type=f32)
        l = jnp.dot(normed, lift_ref[:, q].reshape(part, -1), preferred_element_type=f32)
        gate = g if gate is None else gate + g
        lift = l if lift is None else lift + l
    out_ref[...] = (gate / (1.0 + jnp.exp(-gate)) * lift).astype(bf16)


def down_kernel(act_ref, down_ref, out_ref):
    total = None
    for q in range(NX):
        part = jnp.dot(act_ref[q], down_ref[q], preferred_element_type=f32)
        part = part.astype(bf16).astype(f32)
        total = part if total is None else total + part
    out_ref[...] = total.astype(bf16)


def body(
    context,
    residual_in,
    out_weight,
    norm_gain,
    expert_ids,
    gate_weights,
    gate_matrix,
    lift_matrix,
    down_matrix,
):
    tokens, width = residual_in.shape
    top = expert_ids.shape[1]
    share = width // NX
    piece = share // NZ
    hidden_units = gate_matrix.shape[2]
    capacity = min(tokens, max(2, tokens * top * 9 // (8 * NE)))
    column = NZ * tokens
    rows = ND * NZ * capacity
    x = lax.axis_index("x")

    down_here = down_matrix[0].reshape(hidden_units, NX, share).transpose(1, 0, 2)
    down_here = lax.all_to_all(down_here, "x", split_axis=0, concat_axis=0, tiled=True)

    context_all = lax.all_gather(context, "z", axis=0, tiled=True)
    weight_here = lax.all_gather(out_weight, ("y", "c"), axis=1, tiled=True)
    part = jnp.dot(context_all, weight_here, preferred_element_type=f32)
    attention = lax.psum_scatter(part, "x", scatter_dimension=1, tiled=True)
    residual = lax.dynamic_index_in_dim(
        residual_in.reshape(tokens, NZ, NX, piece), x, 2, keepdims=False
    )
    residual = lax.all_to_all(
        residual.transpose(1, 0, 2), "z", split_axis=0, concat_axis=0, tiled=True
    ).reshape(column, piece)
    hidden_piece = (residual.astype(f32) + attention).astype(bf16)
    hidden_all = lax.all_gather(hidden_piece, "z", axis=0, tiled=False)

    z = lax.axis_index("z")
    own = lax.dynamic_slice_in_dim(hidden_all, z * tokens, tokens, 1)
    own = lax.all_to_all(own, "x", split_axis=0, concat_axis=0, tiled=True)
    own = own.reshape(NX, NZ // NX, tokens, piece).transpose(2, 1, 0, 3).reshape(tokens, share)

    table = pl.pallas_call(
        route_kernel,
        out_shape=jax.ShapeDtypeStruct((NZ, 2 * ND, tokens), f32),
        name="route",
    )(expert_ids.T, gate_weights.T)
    table = lax.all_to_all(table, "z", split_axis=0, concat_axis=0, tiled=True)

    sent = pl.pallas_call(
        functools.partial(dispatch_kernel, capacity),
        out_shape=jax.ShapeDtypeStruct((ND, NZ * capacity, share), bf16),
        compiler_params=params(48),
        name="dispatch",
    )(table, hidden_all)
    received = lax.all_to_all(sent, ("y", "c"), split_axis=0, concat_axis=0, tiled=True)
    gathered = lax.all_gather(received.reshape(rows, share), "x", axis=0, tiled=False)

    block = rows // 4
    gain = norm_gain.astype(f32).reshape(NZ, NX, piece).transpose(1, 0, 2).reshape(NX, share)
    weights = whole(NZ, NX, piece, hidden_units)
    activation = pl.pallas_call(
        functools.partial(up_kernel, width),
        grid=(rows // block,),
        in_specs=[
            pl.BlockSpec((NX, block, share), lambda i: (0, i, 0)),
            whole(NX, share),
            weights,
            weights,
        ],
        out_specs=pl.BlockSpec((block, hidden_units), lambda i: (i, 0)),
        out_shape=jax.ShapeDtypeStruct((rows, hidden_units), bf16),
        compiler_params=params(56),
        name="up",
    )(
        gathered,
        gain,
        gate_matrix.reshape(NZ, NX, piece, hidden_units),
        lift_matrix.reshape(NZ, NX, piece, hidden_units),
    )
    act_all = lax.all_gather(activation, "x", axis=0, tiled=False)
    expert_out = pl.pallas_call(
        down_kernel,
        grid=(rows // block,),
        in_specs=[
            pl.BlockSpec((NX, block, hidden_units), lambda i: (0, i, 0)),
            whole(NX, hidden_units, share),
        ],
        out_specs=pl.BlockSpec((block, share), lambda i: (i, 0)),
        out_shape=jax.ShapeDtypeStruct((rows, share), bf16),
        compiler_params=params(48),
        name="down",
    )(act_all, down_here)
    returned = lax.all_to_all(
        expert_out.reshape(ND, NZ * capacity, share),
        ("y", "c"),
        split_axis=0,
        concat_axis=0,
        tiled=True,
    )
    partial_sum = pl.pallas_call(
        functools.partial(combine_kernel, capacity),
        grid=(ND,),
        in_specs=[
            whole(NZ, 2 * ND, tokens),
            pl.BlockSpec((1, NZ * capacity, share), lambda d: (d, 0, 0)),
        ],
        out_specs=whole(NZ, tokens, share),
        out_shape=jax.ShapeDtypeStruct((NZ, tokens, share), bf16),
        scratch_shapes=[pltpu.VMEM((column, share), f32)],
        compiler_params=params(48),
        name="combine",
    )(table, returned)
    moe = lax.psum_scatter(partial_sum, "z", scatter_dimension=0, tiled=True)
    moe = moe.reshape(tokens, share)
    return (own.astype(f32) + moe.astype(f32)).astype(bf16)


def solution(mesh):
    fine = Mesh(mesh.devices.reshape(NZ, NY, NC, NX), ("z", "y", "c", "x"))
    e = ("z", "y", "c")
    placed = (
        P(e, "x"),
        P(e, None),
        P("x", e),
        P(),
        P(e, None),
        P(e, None),
        P(e, None, "x"),
        P(e, None, "x"),
        P(e, "x", None),
    )
    return jax.shard_map(body, mesh=fine, in_specs=placed, out_specs=P(e, "x"), check_vma=False)
```

```python
import functools

import jax
import jax.numpy as jnp
from jax import lax
from jax.experimental import pallas as pl
from jax.experimental.pallas import tpu as pltpu
from jax.sharding import Mesh
from jax.sharding import PartitionSpec as P

epsilon = 1e-06
f32 = jnp.float32
bf16 = jnp.bfloat16
NZ, NY, NC, NX = 8, 4, 2, 4
NE = NZ * NY * NC
ND = NY * NC
STEPS = (0, 1, 3, 2)
NEAR = (0, 1, -1, 2, -2)
FAR = (3, -3, 4)
TABLE = 32
BY_ROWS = (((0,), (0,)), ((), ()))
BY_COLUMNS = (((1,), (1,)), ((), ()))


def shape(*dims, dtype=bf16):
    return jax.ShapeDtypeStruct(dims, dtype)


def call(kernel, name, outs, *args, scratch=(), mib=32, flops=0, grid=(), specs=None):
    size = sum(a.size * a.dtype.itemsize for a in args)
    blocks = {} if specs is None else dict(grid=grid, in_specs=specs[0], out_specs=specs[1])
    return pl.pallas_call(
        kernel,
        out_shape=outs,
        scratch_shapes=scratch,
        **blocks,
        compiler_params=pltpu.CompilerParams(vmem_limit_bytes=mib << 20),
        cost_estimate=pl.CostEstimate(flops=flops, bytes_accessed=size, transcendentals=0),
        name=name,
    )(*args)


def shift(value, axis, count, step):
    return lax.ppermute(value, axis, [(i, (i + step) % count) for i in range(count)])


def shift_across(value, step):
    pairs = [
        (y * NC + c, ((y + step) % NY) * NC + 1 - c) for y in range(NY) for c in range(NC)
    ]
    return lax.ppermute(value, ("y", "c"), pairs)


def z_ring(value):
    pieces = {0: value}
    right = left = value
    for k in (1, 2, 3):
        right, left = shift(right, "z", NZ, 1), shift(left, "z", NZ, -1)
        pieces[k], pieces[-k] = right, left
    half = value.shape[0] // 2
    pieces[4] = (shift(right[:half], "z", NZ, 1), shift(left[half:], "z", NZ, -1))
    return pieces


def x_ring(value, forward):
    right, left = shift(value, "x", NX, 1), shift(value, "x", NX, -1)
    far = shift(right, "x", NX, 1) if forward else shift(left, "x", NX, -1)
    return value, right, left, far


def route_kernel(ids_ref, gates_ref, residual_ref, out_ref):
    tokens = ids_ref.shape[1]
    piece = out_ref.shape[2]
    x = lax.axis_index("x")
    experts = lax.broadcasted_iota(jnp.int32, (NE, tokens), 0)
    chosen = jnp.zeros((NE, tokens), f32)
    weight = jnp.zeros((NE, tokens), f32)
    for k in range(ids_ref.shape[0]):
        same = experts == ids_ref[k : k + 1, :]
        chosen = jnp.where(same, 1.0, chosen)
        weight = jnp.where(same, gates_ref[k : k + 1, :], weight)
    rows = lax.broadcasted_iota(jnp.int32, (tokens, tokens), 0)
    columns = lax.broadcasted_iota(jnp.int32, (tokens, tokens), 1)
    before = jnp.where(rows < columns, 1.0, 0.0).astype(bf16)
    rank = jnp.dot(chosen.astype(bf16), before, preferred_element_type=f32)
    slot = jnp.where(chosen > 0.0, rank, -1.0)
    high = weight.astype(bf16).astype(f32)
    low = weight - high
    for z in range(NZ):
        column = pl.multiple_of((z * NX + x) * piece, piece)
        out_ref[z, :tokens, :] = residual_ref[:, pl.ds(column, piece)]
        part = [t[z * ND : (z + 1) * ND] for t in (slot, high, low)]
        part.append(jnp.zeros((ND, tokens), f32))
        out_ref[z, tokens:, :] = jnp.concatenate(part, axis=0).astype(bf16)


def project_kernel(count, *refs):
    pieces, weight_ref, outs = refs[:count], refs[count], refs[count + 1 :]
    piece = outs[0].shape[2]
    x = lax.axis_index("x")
    for step, out_ref in zip(STEPS, outs):
        q = lax.rem(x + step, NX)
        weight = weight_ref[pl.ds(pl.multiple_of(q * piece, piece), piece), :]
        block = row = 0
        for ref in pieces:
            part = lax.dot_general(ref[...], weight, BY_COLUMNS, preferred_element_type=f32)
            out_ref[block, row : row + ref.shape[0], :] = part
            row += ref.shape[0]
            if row == out_ref.shape[1]:
                block, row = block + 1, 0


def hidden_kernel(*refs):
    near, far, packed_ref, out_ref = refs[:NX], refs[NX : 2 * NX], refs[2 * NX], refs[2 * NX + 1]
    tokens = out_ref.shape[1]
    z = lax.axis_index("z")
    for group, offsets in ((near, NEAR), (far, FAR)):
        for i, k in enumerate(offsets):
            block = lax.rem(z + NZ - k, NZ)
            total = (group[0][i] + group[1][i]) + (group[2][i] + group[3][i])
            residual = packed_ref[block, :tokens, :].astype(f32)
            out_ref[block] = (residual + total).astype(bf16)


def places(table_ref, d, capacity):
    parts = []
    for z in range(NZ):
        slot = table_ref[z, pl.ds(d, 1), :]
        parts.append(jnp.where(slot >= 0.0, slot + float(z * capacity), -1.0))
    return jnp.concatenate(parts, axis=1).astype(jnp.int32)


def experts_at(step):
    y, c = lax.axis_index("y"), lax.axis_index("c")
    first = lax.rem(y + step, NY) * NC
    return first + c, first + 1 - c


def dispatch_kernel(capacity, packed_ref, *refs):
    pieces = refs[: NZ + 1]
    sent, own = refs[NZ + 1 : NZ + 1 + ND], refs[NZ + 1 + ND : NZ + 1 + ND + NX]
    all_ref, table_ref = refs[-2:]
    tokens = packed_ref.shape[2]
    piece = pieces[0].shape[1]
    x, z = lax.axis_index("x"), lax.axis_index("z")
    row = 0
    for ref, k in zip(pieces, (0, 1, -1, 2, -2, 3, -3, 4, 4)):
        block = lax.rem(z + NZ - k, NZ)
        column = pl.multiple_of(block * piece, piece)
        size = ref.shape[0]
        all_ref[row : row + size, pl.ds(column, piece)] = ref[...]
        row = (row + size) % all_ref.shape[0]
    for i in range(NZ):
        table_ref[i] = packed_ref[i, tokens:, :].astype(f32)
    slots = lax.broadcasted_iota(jnp.int32, (NZ * capacity, NZ * tokens), 0)
    for i, step in enumerate(STEPS):
        for j, d in enumerate(experts_at(step)):
            pick = jnp.where(slots == places(table_ref, d, capacity), 1.0, 0.0).astype(bf16)
            out_ref = sent[NC * i + j]

            @pl.loop(0, all_ref.shape[1] // 256)
            def _(n, pick=pick, out_ref=out_ref):
                span = pl.ds(pl.multiple_of(n * 256, 256), 256)
                rows = jnp.dot(pick, all_ref[:, span], preferred_element_type=f32)
                out_ref[:, span] = rows.astype(bf16)

    mine = pl.ds(pl.multiple_of(z * tokens, tokens), tokens)
    per = NZ // NX
    for ref, step in zip(own, STEPS):
        first = lax.rem(x + step, NX) * per
        for b in range(per):
            ref[b] = all_ref[mine, pl.ds(pl.multiple_of((first + b) * piece, piece), piece)]


def up_kernel(width, *refs):
    pieces, (gain_ref, gate_ref, lift_ref, out_ref, gate_acc, lift_acc) = refs[:NX], refs[NX:]
    share = pieces[0].shape[1]
    x = lax.axis_index("x")
    squares = None
    for ref in pieces:
        h = ref[...].astype(f32)
        s = jnp.sum(h * h, axis=1, keepdims=True)
        squares = s if squares is None else squares + s
    scale = lax.rsqrt(squares * (1.0 / width) + epsilon)
    depth = 2 * gate_ref.shape[2]
    gate_acc[...] = jnp.zeros_like(gate_acc)
    lift_acc[...] = jnp.zeros_like(lift_acc)
    for ref, back in zip(pieces, STEPS):
        q = lax.rem(x + NX - back, NX)

        @pl.loop(0, share // depth)
        def _(k, ref=ref, q=q):
            span = pl.ds(pl.multiple_of(k * depth, depth), depth)
            normed = ref[:, span].astype(f32) * scale * gain_ref[pl.ds(q, 1), span]
            normed = normed.astype(bf16)
            for weight_ref, acc in ((gate_ref, gate_acc), (lift_ref, lift_acc)):
                weight = weight_ref[pl.ds(2 * k, 2), q].reshape(depth, -1)
                acc[...] += jnp.dot(normed, weight, preferred_element_type=f32)

    gate = gate_acc[...]
    out_ref[...] = (gate / (1.0 + jnp.exp(-gate)) * lift_acc[...]).astype(bf16)


def down_kernel(*refs):
    acts, downs, outs = refs[:NX], refs[NX : 2 * NX], refs[2 * NX :]
    total = None
    for act, down in zip(acts, downs):
        part = jnp.dot(act[...], down[...], preferred_element_type=f32)
        part = part.astype(bf16).astype(f32)
        total = part if total is None else total + part
    total = total.astype(bf16)
    rows = outs[0].shape[0]
    for i, out in enumerate(outs):
        out[...] = total[i * rows : (i + 1) * rows]


def combine_kernel(capacity, step, packed_ref, own_ref, other_ref, *refs):
    table_ref, out_ref = refs[-1], refs[-2]
    tokens = packed_ref.shape[2]
    z = pl.program_id(0)
    table_ref[...] = packed_ref[0].astype(f32)
    first = (z * capacity) // 16 * 16
    window = pl.ds(pl.multiple_of(first, 16), 32)
    offset = z * capacity - first
    slots = lax.broadcasted_iota(jnp.int32, (32, tokens), 0) - offset
    slots = slots.astype(f32)
    spread, rows = [], []
    for d, ref in zip(experts_at(step), (own_ref, other_ref)):
        hit = slots == table_ref[pl.ds(d, 1), :]
        hit = hit & (slots >= 0.0)
        for part in (1, 2):
            gate = table_ref[pl.ds(part * ND + d, 1), :]
            spread.append(jnp.where(hit, gate, 0.0))
            rows.append(ref[window, :])
    total = lax.dot_general(
        jnp.concatenate(spread, axis=0).astype(bf16),
        jnp.concatenate(rows, axis=0),
        BY_ROWS,
        preferred_element_type=f32,
    )
    if len(refs) == 3:
        total = total + refs[0][0]
    out_ref[0] = total.astype(out_ref.dtype)


def final_kernel(moe_ref, *refs):
    own, out_ref = refs[:NX], refs[NX]
    piece = own[0].shape[2]
    x = lax.axis_index("x")
    for ref, step in zip(own, STEPS):
        owner = lax.rem(x + NX - step, NX)
        for b in range(ref.shape[0]):
            column = pl.multiple_of((b * NX + owner) * piece, piece)
            total = moe_ref[0, :, pl.ds(column, piece)].astype(f32)
            for i in range(1, NZ):
                total = total + moe_ref[i, :, pl.ds(column, piece)].astype(f32)
            out_ref[:, pl.ds(column, piece)] = (ref[b].astype(f32) + total).astype(bf16)


def body(
    context,
    residual_in,
    out_weight,
    norm_gain,
    expert_ids,
    gate_weights,
    gate_matrix,
    lift_matrix,
    down_matrix,
):
    tokens, width = residual_in.shape
    top = expert_ids.shape[1]
    share = width // NX
    piece = share // NZ
    units = gate_matrix.shape[2]
    capacity = min(tokens, max(2, tokens * top * 9 // (8 * NE)))
    column = NZ * tokens
    slots = NZ * capacity
    x = lax.axis_index("x")

    packed = call(
        route_kernel,
        "route",
        shape(NZ, tokens + TABLE, piece),
        expert_ids.T,
        gate_weights.T,
        residual_in,
    )
    weight = lax.all_gather(out_weight.T, ("y", "c"), axis=0, tiled=True)
    ring = z_ring(context)
    near = call(
        functools.partial(project_kernel, len(NEAR)),
        "project_near",
        [shape(len(NEAR), tokens, piece, dtype=f32)] * NX,
        *[ring[k] for k in NEAR],
        weight,
        flops=2 * len(NEAR) * tokens * share * NX * piece,
    )
    far = call(
        functools.partial(project_kernel, len(FAR) + 1),
        "project_far",
        [shape(len(FAR), tokens, piece, dtype=f32)] * NX,
        *[ring[k] for k in FAR[:-1]],
        *ring[4],
        weight,
        flops=2 * len(FAR) * tokens * share * NX * piece,
    )
    packed, far = lax.optimization_barrier((packed, far))
    packed = lax.all_to_all(packed, "z", split_axis=0, concat_axis=0, tiled=True)
    near = [near[0]] + [shift(p, "x", NX, s) for p, s in zip(near[1:], STEPS[1:])]
    far = [far[0]] + [shift(p, "x", NX, s) for p, s in zip(far[1:], STEPS[1:])]
    hidden = call(
        hidden_kernel, "hidden", shape(NZ, tokens, piece), *near, *far, packed
    ).reshape(column, piece)

    down_here, hidden = lax.optimization_barrier((down_matrix[0], hidden))
    downs = [
        lax.dynamic_slice_in_dim(down_here, lax.rem(x + s, NX) * share, share, 1) for s in STEPS
    ]
    downs = [downs[0]] + [shift(p, "x", NX, s) for p, s in zip(downs[1:], STEPS[1:])]

    ring = z_ring(hidden)
    sent = call(
        functools.partial(dispatch_kernel, capacity),
        "dispatch",
        [shape(slots, share)] * ND + [shape(NZ // NX, tokens, piece)] * NX,
        packed,
        *[ring[k] for k in NEAR],
        *[ring[k] for k in FAR[:-1]],
        *ring[4],
        scratch=[pltpu.VMEM((column, share), bf16), pltpu.VMEM((NZ, TABLE, tokens), f32)],
        flops=2 * ND * slots * column * share,
    )
    sent, downs = lax.optimization_barrier((sent, downs))
    own = sent[ND:]
    own = [own[0]] + [shift(p, "x", NX, s) for p, s in zip(own[1:], STEPS[1:])]

    gain = norm_gain.astype(f32).reshape(NZ, NX, piece).transpose(1, 0, 2).reshape(NX, share)
    gate_here = gate_matrix.reshape(NZ, NX, piece, units)
    lift_here = lift_matrix.reshape(NZ, NX, piece, units)
    total = None
    for i, step in enumerate(STEPS):
        near_rows, far_rows = sent[NC * i : NC * i + NC]
        if step:
            near_rows = shift(near_rows, "y", NY, step)
        far_rows = shift_across(far_rows, step)
        rows = jnp.concatenate([near_rows, far_rows], axis=0)
        rows = x_ring(rows, i % 2 == 0)
        act = call(
            functools.partial(up_kernel, width),
            f"up{step}",
            shape(NC * slots, units),
            *rows,
            gain,
            gate_here,
            lift_here,
            scratch=[pltpu.VMEM((NC * slots, units), f32)] * 2,
            flops=4 * NC * slots * width * units,
        )
        acts = x_ring(act, i % 2 == 0)
        back = call(
            down_kernel,
            f"down{step}",
            [shape(slots, share)] * NC,
            *acts,
            *downs,
            flops=2 * NC * slots * NX * units * share,
            grid=(share // 256,),
            specs=(
                [pl.BlockSpec((NC * slots, units), lambda i: (0, 0))] * NX
                + [pl.BlockSpec((units, 256), lambda i: (0, i))] * NX,
                [pl.BlockSpec((slots, 256), lambda i: (0, i))] * NC,
            ),
        )
        near_rows, far_rows = back
        if step:
            near_rows = shift(near_rows, "y", NY, -step)
        far_rows = shift_across(far_rows, -step)
        last = i == len(STEPS) - 1
        block = pl.BlockSpec((1, tokens, share), lambda z: (z, 0, 0))
        rows = pl.BlockSpec((slots, share), lambda z: (0, 0))
        table = pl.BlockSpec((1, TABLE, piece), lambda z: (z, tokens // TABLE, 0))
        total = call(
            functools.partial(combine_kernel, capacity, step),
            f"combine{step}",
            shape(NZ, tokens, share, dtype=bf16 if last else f32),
            packed,
            near_rows,
            far_rows,
            *([] if total is None else [total]),
            scratch=[pltpu.VMEM((TABLE, tokens), f32)],
            flops=4 * NC * NZ * 32 * tokens * share,
            grid=(NZ,),
            specs=([table, rows, rows] + ([] if total is None else [block]), block),
        )
    moe = lax.all_to_all(total, "z", split_axis=0, concat_axis=0, tiled=True)
    return call(final_kernel, "final", shape(tokens, share), moe, *own)


def solution(mesh):
    fine = Mesh(mesh.devices.reshape(NZ, NY, NC, NX), ("z", "y", "c", "x"))
    e = ("z", "y", "c")
    placed = (
        P(e, "x"),
        P(e, None),
        P("x", e),
        P(),
        P(e, None),
        P(e, None),
        P(e, None, "x"),
        P(e, None, "x"),
        P(e, "x", None),
    )
    return jax.shard_map(body, mesh=fine, in_specs=placed, out_specs=P(e, "x"), check_vma=False)
```

```python
import functools

import jax
import jax.numpy as jnp
from jax import lax
from jax.experimental import pallas as pl
from jax.experimental.pallas import tpu as pltpu
from jax.sharding import Mesh
from jax.sharding import PartitionSpec as P

epsilon = 1e-06
f32 = jnp.float32
bf16 = jnp.bfloat16
NZ, NY, NC, NX = 8, 4, 2, 4
NE = NZ * NY * NC
STEPS = (0, 1, 3, 2)
GROUPS = ((0,), (1, -1), (3, -3, 4), (2, -2))
SHIFTS = sum(GROUPS, ())
TABLE = 32
BY_ROWS = (((0,), (0,)), ((), ()))
BY_COLUMNS = (((1,), (1,)), ((), ()))


def shape(*dims, dtype=bf16):
    return jax.ShapeDtypeStruct(dims, dtype)


def call(kernel, name, outs, *args, scratch=(), mib=40, flops=0, grid=(), specs=None):
    size = sum(a.size * a.dtype.itemsize for a in args)
    blocks = {} if specs is None else dict(grid=grid, in_specs=specs[0], out_specs=specs[1])
    return pl.pallas_call(
        kernel,
        out_shape=outs,
        scratch_shapes=scratch,
        **blocks,
        compiler_params=pltpu.CompilerParams(vmem_limit_bytes=mib << 20),
        cost_estimate=pl.CostEstimate(flops=flops, bytes_accessed=size, transcendentals=0),
        name=name,
    )(*args)


def shift(value, axis, count, step):
    if step % count == 0:
        return value
    return lax.ppermute(value, axis, [(i, (i + step) % count) for i in range(count)])


def y_exchange(values):
    return [shift(v, "y", NY, s) for v, s in zip(values, STEPS)]


def x_exchange(values):
    return [shift(v, "x", NX, s) for v, s in zip(values, STEPS)]


def swap(value):
    return shift(value, "c", NC, 1)


def x_ring(value, forward):
    right, left = shift(value, "x", NX, 1), shift(value, "x", NX, -1)
    far = shift(right, "x", NX, 1) if forward else shift(left, "x", NX, -1)
    return value, right, left, far


def route_kernel(ids_ref, gates_ref, residual_ref, *outs):
    tokens = ids_ref.shape[1]
    x, y = lax.axis_index("x"), lax.axis_index("y")
    row = lax.broadcasted_iota(jnp.int32, (NE, tokens), 0)
    group = row // (NC * NZ)
    step = group ^ (group >> 1)
    experts = (row % NZ) * (NY * NC) + ((y + step) % NY) * NC + (row // NZ) % NC
    chosen = jnp.zeros((NE, tokens), f32)
    weight = jnp.zeros((NE, tokens), f32)
    for k in range(ids_ref.shape[0]):
        same = experts == ids_ref[k : k + 1, :]
        chosen = jnp.where(same, 1.0, chosen)
        weight = jnp.where(same, gates_ref[k : k + 1, :], weight)
    rows = lax.broadcasted_iota(jnp.int32, (tokens, tokens), 0)
    columns = lax.broadcasted_iota(jnp.int32, (tokens, tokens), 1)
    before = jnp.where(rows < columns, 1.0, 0.0).astype(bf16)
    rank = jnp.dot(chosen.astype(bf16), before, preferred_element_type=f32)
    slot = jnp.where(chosen > 0.0, rank, -1.0)
    high = weight.astype(bf16).astype(f32)
    low = weight - high
    share = residual_ref.shape[1] // NX
    half, piece = share // 2, share // 8
    for i, (s, out_ref) in enumerate(zip(STEPS, outs)):
        there = lax.rem(y + s, NY)
        for b in range(2):
            column = pl.multiple_of(x * share + b * half + there * piece, piece)
            out_ref[:tokens, b * piece : (b + 1) * piece] = residual_ref[:, pl.ds(column, piece)]
        for c in range(NC):
            at = (i * NC + c) * NZ
            part = [t[at : at + NZ] for t in (slot, high, low)]
            part.append(jnp.zeros((NZ, tokens), f32))
            part = jnp.concatenate(part, axis=0).astype(bf16)
            out_ref[tokens:, c * tokens : (c + 1) * tokens] = part


def project_kernel(*refs):
    contexts, weight_ref, outs = refs[:NY], refs[NY], refs[NY + 1 :]
    x = lax.axis_index("x")
    for step, out_ref in zip(STEPS, outs):
        q = lax.rem(x + step, NX)
        weight = weight_ref[pl.ds(2 * q, 2)].reshape(out_ref.shape[2], -1)
        for i, ref in enumerate(contexts):
            part = lax.dot_general(ref[...], weight, BY_COLUMNS, preferred_element_type=f32)
            out_ref[i] = part.astype(out_ref.dtype)


def hidden_kernel(*refs):
    parts, packed, out_ref = refs[:NX], refs[NX : NX + NY], refs[NX + NY]
    tokens = parts[0].shape[1]
    y = lax.axis_index("y")
    for i, s in enumerate(STEPS):
        total = parts[0][i]
        for ref in parts[1:]:
            total = total + ref[i].astype(f32)
        owner = lax.rem(y + NY - s, NY)
        residual = packed[i][:tokens, :].astype(f32)
        out_ref[pl.ds(pl.multiple_of(owner * tokens, tokens), tokens), :] = (
            residual + total
        ).astype(bf16)


def fill_table(packed, other_ref, table_ref):
    tokens = table_ref.shape[2]
    y, c = lax.axis_index("y"), lax.axis_index("c")
    mine = pl.ds(pl.multiple_of(c * tokens, tokens), tokens)
    for i, s in enumerate(STEPS):
        owner = lax.rem(y + NY - s, NY)
        table_ref[owner] = packed[i][-TABLE:, mine].astype(f32)
        table_ref[owner + NY] = other_ref[i].astype(f32)


def pick_kernel(*refs):
    packed, out_ref = refs[:NY], refs[NY]
    tokens = out_ref.shape[2]
    c = lax.axis_index("c")
    others = pl.ds(pl.multiple_of((1 - c) * tokens, tokens), tokens)
    for i in range(NY):
        out_ref[i] = packed[i][-TABLE:, others]


def gather_kernel(*refs):
    pieces, out_ref = refs[:NY], refs[NY]
    y = lax.axis_index("y")
    piece = pieces[0].shape[1] // 2
    half = out_ref.shape[1] // 2
    for ref, s in zip(pieces, STEPS):
        owner = lax.rem(y + NY - s, NY)
        for b in range(2):
            column = pl.multiple_of(b * half + owner * piece, piece)
            out_ref[:, pl.ds(column, piece)] = ref[:, b * piece : (b + 1) * piece]


def dispatch_kernel(capacity, *refs):
    packed, other_ref = refs[:NY], refs[NY]
    hidden_ref, across_ref = refs[NY + 1 : NY + 3]
    sent, (own_ref, table_out, table_ref) = refs[NY + 3 : -3], refs[-3:]
    tokens = own_ref.shape[0]
    blocks = NY * NC
    y, z = lax.axis_index("y"), lax.axis_index("z")
    fill_table(packed, other_ref, table_ref)
    table_out[...] = table_ref[...]
    own_ref[...] = hidden_ref[pl.ds(pl.multiple_of(y * tokens, tokens), tokens), :]
    slots = lax.broadcasted_iota(jnp.int32, (blocks * capacity, NY * tokens), 0)
    for s, out_ref in zip(SHIFTS, sent):
        d = lax.rem(z + NZ + s, NZ)
        rows = None
        for core, ref in enumerate((hidden_ref, across_ref)):
            parts = []
            for b in range(core * NY, core * NY + NY):
                slot = table_ref[b, pl.ds(d, 1), :]
                parts.append(jnp.where(slot >= 0.0, slot + float(b * capacity), -1.0))
            place = jnp.concatenate(parts, axis=1).astype(jnp.int32)
            pick = jnp.where(slots == place, 1.0, 0.0).astype(bf16)
            part = jnp.dot(pick, ref[...], preferred_element_type=f32)
            rows = part if rows is None else rows + part
        out_ref[...] = rows.astype(bf16)


def up_kernel(width, *refs):
    pieces, (gain_ref, gate_ref, lift_ref, out_ref) = refs[:NX], refs[NX:]
    x = lax.axis_index("x")
    squares = None
    for ref in pieces:
        h = ref[...].astype(f32)
        s = jnp.sum(h * h, axis=1, keepdims=True)
        squares = s if squares is None else squares + s
    scale = lax.rsqrt(squares * (1.0 / width) + epsilon)
    gate = lift = None
    for ref, back in zip(pieces, STEPS):
        q = lax.rem(x + NX - back, NX)
        normed = (ref[...].astype(f32) * scale * gain_ref[pl.ds(q, 1), :]).astype(bf16)
        g = jnp.dot(normed, gate_ref[q], preferred_element_type=f32)
        l = jnp.dot(normed, lift_ref[q], preferred_element_type=f32)
        gate = g if gate is None else gate + g
        lift = l if lift is None else lift + l
    out_ref[...] = (gate / (1.0 + jnp.exp(-gate)) * lift).astype(bf16)


def down_kernel(*refs):
    acts, downs, outs = refs[:NX], refs[NX : 2 * NX], refs[2 * NX :]
    total = None
    for act, down in zip(acts, downs):
        part = jnp.dot(act[...], down[...], preferred_element_type=f32)
        part = part.astype(bf16).astype(f32)
        total = part if total is None else total + part
    total = total.astype(bf16)
    rows = outs[0].shape[0]
    for i, out in enumerate(outs):
        out[...] = total[i * rows : (i + 1) * rows]


def combine_kernel(capacity, start, shifts, table_ref, *refs):
    lists, rest, out_ref = refs[: len(shifts)], refs[len(shifts) : -1], refs[-1]
    tokens = table_ref.shape[2]
    block = pl.program_id(0) + start
    z = lax.axis_index("z")
    first = (block * capacity) // 16 * 16
    window = pl.ds(pl.multiple_of(first, 16), 32)
    slots = lax.broadcasted_iota(jnp.int32, (32, tokens), 0) - (block * capacity - first)
    slots = slots.astype(f32)
    spread, rows = [], []
    for s, ref in zip(shifts, lists):
        d = lax.rem(z + NZ + s, NZ)
        hit = (slots == table_ref[0, pl.ds(d, 1), :]) & (slots >= 0.0)
        for part in (1, 2):
            gate = table_ref[0, pl.ds(part * NZ + d, 1), :]
            spread.append(jnp.where(hit, gate, 0.0))
            rows.append(ref[window, :])
    total = lax.dot_general(
        jnp.concatenate(spread, axis=0).astype(bf16),
        jnp.concatenate(rows, axis=0),
        BY_ROWS,
        preferred_element_type=f32,
    )
    if rest:
        total = total + rest[0][0]
    out_ref[0] = total.astype(out_ref.dtype)


def merge_kernel(own_ref, got_ref, *outs):
    y = lax.axis_index("y")
    for s, out_ref in zip(STEPS, outs):
        there = lax.rem(y + s, NY)
        out_ref[...] = (own_ref[there] + got_ref[there].astype(f32)).astype(out_ref.dtype)


def final_kernel(hidden_ref, *refs):
    total = refs[0][...]
    for ref in refs[1:-1]:
        total = total + ref[...].astype(f32)
    refs[-1][...] = (hidden_ref[...].astype(f32) + total).astype(bf16)


def body(
    context,
    residual_in,
    out_weight,
    norm_gain,
    expert_ids,
    gate_weights,
    gate_matrix,
    lift_matrix,
    down_matrix,
):
    tokens, width = residual_in.shape
    top = expert_ids.shape[1]
    share = width // NX
    fine = share // NY
    units = gate_matrix.shape[2]
    capacity = min(tokens, max(2, tokens * top * 9 // (8 * NE)))
    blocks = NY * NC
    slots = blocks * capacity
    x = lax.axis_index("x")

    weight = lax.all_gather(out_weight.T, ("z", "c"), axis=0, tiled=True)
    weight = weight.reshape(NZ, -1, share)
    contexts = [shift(context, "y", NY, s) for s in STEPS]
    downs = [
        lax.dynamic_slice_in_dim(down_matrix[0], lax.rem(x + s, NX) * share, share, 1)
        for s in STEPS
    ]
    downs = x_exchange(downs)
    packed = call(
        route_kernel,
        "route",
        [shape(tokens + TABLE, fine)] * NY,
        expert_ids.T,
        gate_weights.T,
        residual_in,
    )
    packed = y_exchange(packed)
    table = swap(call(pick_kernel, "pick", shape(NY, TABLE, tokens), *packed))
    contexts, downs, packed, table = lax.optimization_barrier((contexts, downs, packed, table))
    parts = call(
        project_kernel,
        "project",
        [shape(NY, tokens, fine, dtype=f32)] + [shape(NY, tokens, fine)] * (NX - 1),
        *contexts,
        weight,
        flops=2 * NY * tokens * share * width // NY,
    )
    parts = x_exchange(parts)
    hidden = call(hidden_kernel, "hidden", shape(NY * tokens, fine), *parts, *packed)
    pieces = [shift(hidden, "y", NY, s) for s in STEPS]
    hidden = call(gather_kernel, "gather", shape(NY * tokens, share), *pieces)
    *sent, own, table = call(
        functools.partial(dispatch_kernel, capacity),
        "dispatch",
        [shape(slots, share)] * NZ
        + [shape(tokens, share), shape(blocks, TABLE, tokens, dtype=f32)],
        *packed,
        table,
        hidden,
        swap(hidden),
        scratch=[pltpu.VMEM((blocks, TABLE, tokens), f32)],
        flops=2 * NZ * slots * blocks * tokens * share,
    )

    gain = norm_gain.astype(f32).reshape(NX, share)
    gate_here = gate_matrix.reshape(NX, share, units)
    lift_here = lift_matrix.reshape(NX, share, units)

    sent = dict(zip(SHIFTS, sent))
    got, rings, acts = [], [], []
    for i, group in enumerate(GROUPS):
        rows = [sent[s] for s in group]
        if i == len(GROUPS) - 1:
            rows, got[1] = lax.optimization_barrier((rows, got[1]))
        rows = [shift(r, "z", NZ, s) for r, s in zip(rows, group)]
        got.append(rows[0] if len(rows) == 1 else jnp.concatenate(rows, axis=0))
    for i, group in enumerate(GROUPS):
        rows = got[i]
        if i >= 2:
            rows, acts[i - 2] = lax.optimization_barrier((rows, acts[i - 2]))
        count = rows.shape[0]
        ring = x_ring(rows, i % 2 == 0)
        acts.append(
            call(
                functools.partial(up_kernel, width),
                f"up{i}",
                shape(count, units),
                *ring,
                gain,
                gate_here,
                lift_here,
                flops=4 * count * width * units,
            )
        )
    total = None
    for i, group in enumerate(GROUPS):
        count = got[i].shape[0]
        back = call(
            down_kernel,
            f"down{i}",
            [shape(slots, share)] * len(group),
            *x_ring(acts[i], i % 2 == 0),
            *downs,
            flops=2 * count * NX * units * share,
            grid=(share // 256,),
            specs=(
                [pl.BlockSpec((count, units), lambda i: (0, 0))] * NX
                + [pl.BlockSpec((units, 256), lambda i: (0, i))] * NX,
                [pl.BlockSpec((slots, 256), lambda i: (0, i))] * len(group),
            ),
        )
        lists = [shift(r, "z", NZ, -s) for r, s in zip(back, group)]

        def combine(start, number, dtype, total=total, lists=lists, group=group, i=i):
            part = pl.BlockSpec((1, tokens, share), lambda b: (b, 0, 0))
            there = pl.BlockSpec((1, tokens, share), lambda b: (b + start, 0, 0))
            return call(
                functools.partial(combine_kernel, capacity, start, group),
                f"combine{i}_{start}",
                shape(number, tokens, share, dtype=dtype),
                table,
                *lists,
                *([] if total is None else [total]),
                flops=4 * len(group) * number * 32 * tokens * share,
                grid=(number,),
                specs=(
                    [pl.BlockSpec((1, TABLE, tokens), lambda b: (b + start, 0, 0))]
                    + [pl.BlockSpec((slots, share), lambda b: (0, 0))] * len(group)
                    + ([] if total is None else [there]),
                    part,
                ),
            )

        if i < len(GROUPS) - 1:
            total = combine(0, blocks, f32)
    crossing = combine(NY, NY, bf16)
    mine = combine(0, NY, f32)
    merged = call(
        merge_kernel,
        "merge",
        [shape(tokens, share, dtype=f32)] + [shape(tokens, share)] * (NY - 1),
        mine,
        swap(crossing),
    )
    return call(final_kernel, "final", shape(tokens, share), own, *y_exchange(merged))


def solution(mesh):
    fine = Mesh(mesh.devices.reshape(NZ, NY, NC, NX), ("z", "y", "c", "x"))
    e = ("z", "y", "c")
    placed = (
        P(e, "x"),
        P(e, None),
        P("x", e),
        P(),
        P(e, None),
        P(e, None),
        P(e, None, "x"),
        P(e, None, "x"),
        P(e, "x", None),
    )
    return jax.shard_map(body, mesh=fine, in_specs=placed, out_specs=P(e, "x"), check_vma=False)
```

```python
import functools

import jax
import jax.numpy as jnp
from jax import lax
from jax.experimental import pallas as pl
from jax.experimental.pallas import tpu as pltpu
from jax.sharding import Mesh
from jax.sharding import PartitionSpec as P

epsilon = 1e-06
f32 = jnp.float32
bf16 = jnp.bfloat16
NZ, NY, NC, NX = 8, 4, 2, 4
NE = NZ * NY * NC
STEPS = (0, 1, 3, 2)
CHUNKS = 3
RING = (0, 1, -1, 2, -2, 3, -3)
TABLE = 32
BY_ROWS = (((0,), (0,)), ((), ()))
BY_COLUMNS = (((1,), (1,)), ((), ()))


def shape(*dims, dtype=bf16):
    return jax.ShapeDtypeStruct(dims, dtype)


def call(kernel, name, outs, *args, scratch=(), mib=40, flops=0, grid=(), specs=None):
    size = sum(a.size * a.dtype.itemsize for a in args)
    blocks = {} if specs is None else dict(grid=grid, in_specs=specs[0], out_specs=specs[1])
    return pl.pallas_call(
        kernel,
        out_shape=outs,
        scratch_shapes=scratch,
        **blocks,
        compiler_params=pltpu.CompilerParams(vmem_limit_bytes=mib << 20),
        cost_estimate=pl.CostEstimate(flops=flops, bytes_accessed=size, transcendentals=0),
        name=name,
    )(*args)


def shift(value, axis, count, step):
    if step % count == 0:
        return value
    return lax.ppermute(value, axis, [(i, (i + step) % count) for i in range(count)])


def y_exchange(values):
    return [shift(v, "y", NY, s) for v, s in zip(values, STEPS)]


def x_exchange(values):
    return [shift(v, "x", NX, s) for v, s in zip(values, STEPS)]


def swap(value):
    return shift(value, "c", NC, 1)


def x_ring(value, way):
    right, left = shift(value, "x", NX, 1), shift(value, "x", NX, -1)
    right, left = lax.optimization_barrier((right, left))
    half = value.shape[0] // 2
    if way == 0:
        far = shift(right, "x", NX, 1)
    elif way == 1:
        far = shift(left, "x", NX, -1)
    else:
        far = shift(right[:half], "x", NX, 1), shift(left[half:], "x", NX, -1)
        far = jnp.concatenate(far, axis=0)
    return value, right, left, far


def z_ring(value):
    right = left = value
    pieces = [value]
    for _ in range(NZ // 2 - 1):
        right, left = shift(right, "z", NZ, 1), shift(left, "z", NZ, -1)
        pieces += [right, left]
    half = value.shape[0] // 2
    return pieces + [shift(right[:half], "z", NZ, 1), shift(left[half:], "z", NZ, -1)]


def z_exchange(value):
    return lax.all_to_all(value, "z", split_axis=0, concat_axis=0, tiled=True)


def route_kernel(ids_ref, gates_ref, residual_ref, *outs):
    tokens = ids_ref.shape[1]
    x, y = lax.axis_index("x"), lax.axis_index("y")
    row = lax.broadcasted_iota(jnp.int32, (NE, tokens), 0)
    group = row // (NC * NZ)
    step = group ^ (group >> 1)
    experts = (row % NZ) * (NY * NC) + ((y + step) % NY) * NC + (row // NZ) % NC
    chosen = jnp.zeros((NE, tokens), f32)
    weight = jnp.zeros((NE, tokens), f32)
    for k in range(ids_ref.shape[0]):
        same = experts == ids_ref[k : k + 1, :]
        chosen = jnp.where(same, 1.0, chosen)
        weight = jnp.where(same, gates_ref[k : k + 1, :], weight)
    rows = lax.broadcasted_iota(jnp.int32, (tokens, tokens), 0)
    columns = lax.broadcasted_iota(jnp.int32, (tokens, tokens), 1)
    before = jnp.where(rows < columns, 1.0, 0.0).astype(bf16)
    rank = jnp.dot(chosen.astype(bf16), before, preferred_element_type=f32)
    slot = jnp.where(chosen > 0.0, rank, -1.0)
    high = weight.astype(bf16).astype(f32)
    low = weight - high
    share = residual_ref.shape[1] // NX
    half, piece = share // 2, share // 8
    for i, (s, out_ref) in enumerate(zip(STEPS, outs)):
        there = lax.rem(y + s, NY)
        for b in range(2):
            column = pl.multiple_of(x * share + b * half + there * piece, piece)
            out_ref[:tokens, b * piece : (b + 1) * piece] = residual_ref[:, pl.ds(column, piece)]
        for c in range(NC):
            at = (i * NC + c) * NZ
            part = [t[at : at + NZ] for t in (slot, high, low)]
            part.append(jnp.zeros((NZ, tokens), f32))
            part = jnp.concatenate(part, axis=0).astype(bf16)
            out_ref[tokens:, c * tokens : (c + 1) * tokens] = part


def project_kernel(*refs):
    contexts, (mine_ref, other_ref), outs = refs[:NY], refs[NY : NY + 2], refs[NY + 2 : -1]
    all_ref = refs[-1]
    width = all_ref.shape[1] // NC
    x, z, c = lax.axis_index("x"), lax.axis_index("z"), lax.axis_index("c")
    for i in range(NZ):
        owner = lax.rem(z + NZ - (RING + (4,))[i], NZ)
        for ref, core in ((mine_ref, c), (other_ref, 1 - c)):
            there = pl.ds(pl.multiple_of(core * width, width), width)
            all_ref[owner, there, :] = ref[i * width : (i + 1) * width, :]
    for step, out_ref in zip(STEPS, outs):
        q = lax.rem(x + step, NX)
        weight = all_ref[pl.ds(2 * q, 2)].reshape(out_ref.shape[2], -1)
        for i, ref in enumerate(contexts):
            part = lax.dot_general(ref[...], weight, BY_COLUMNS, preferred_element_type=f32)
            out_ref[i] = part.astype(out_ref.dtype)


def hidden_kernel(*refs):
    parts, packed, out_ref = refs[:NX], refs[NX : NX + NY], refs[NX + NY]
    tokens = parts[0].shape[1]
    y = lax.axis_index("y")
    for i, s in enumerate(STEPS):
        total = parts[0][i]
        for ref in parts[1:]:
            total = total + ref[i].astype(f32)
        owner = lax.rem(y + NY - s, NY)
        residual = packed[i][:tokens, :].astype(f32)
        out_ref[pl.ds(pl.multiple_of(owner * tokens, tokens), tokens), :] = (
            residual + total
        ).astype(bf16)


def fill_own(packed, table_ref):
    tokens = table_ref.shape[2]
    y, c = lax.axis_index("y"), lax.axis_index("c")
    mine = pl.ds(pl.multiple_of(c * tokens, tokens), tokens)
    for i, s in enumerate(STEPS):
        owner = lax.rem(y + NY - s, NY)
        table_ref[owner] = packed[i][-TABLE:, mine].astype(f32)


def send_rows(capacity, table_ref, hidden, first, out_ref):
    count = out_ref.shape[1]
    tokens = table_ref.shape[2]
    for d in range(NZ):
        rows = None
        for core, ref in hidden:
            parts = []
            for b in range(core * NY, core * NY + NY):
                slot = table_ref[b, d : d + 1, :]
                parts.append(jnp.where(slot >= 0.0, slot + float(b * capacity - first), -1.0))
            place = jnp.concatenate(parts, axis=1).astype(jnp.int32)
            slots = lax.broadcasted_iota(jnp.int32, (count, NY * tokens), 0)
            pick = jnp.where(slots == place, 1.0, 0.0).astype(bf16)
            part = jnp.dot(pick, ref[...], preferred_element_type=f32)
            rows = part if rows is None else rows + part
        out_ref[d] = rows.astype(bf16)


def pick_kernel(*refs):
    packed, out_ref = refs[:NY], refs[NY]
    tokens = out_ref.shape[2]
    c = lax.axis_index("c")
    others = pl.ds(pl.multiple_of((1 - c) * tokens, tokens), tokens)
    for i in range(NY):
        out_ref[i] = packed[i][-TABLE:, others]


def gather_kernel(*refs):
    pieces, out_ref = refs[:NY], refs[NY]
    y = lax.axis_index("y")
    piece = pieces[0].shape[1] // 2
    half = out_ref.shape[1] // 2
    for ref, s in zip(pieces, STEPS):
        owner = lax.rem(y + NY - s, NY)
        for b in range(2):
            column = pl.multiple_of(b * half + owner * piece, piece)
            out_ref[:, pl.ds(column, piece)] = ref[:, b * piece : (b + 1) * piece]


def dispatch_own_kernel(capacity, *refs):
    packed, (hidden_ref, out_ref, own_ref, table_ref) = refs[:NY], refs[NY:]
    tokens = own_ref.shape[0]
    y = lax.axis_index("y")
    fill_own(packed, table_ref)
    own_ref[...] = hidden_ref[pl.ds(pl.multiple_of(y * tokens, tokens), tokens), :]
    send_rows(capacity, table_ref, ((0, hidden_ref),), 0, out_ref)


def dispatch_kernel(capacity, *refs):
    packed, (other_ref, hidden_ref, across_ref) = refs[:NY], refs[NY : NY + 3]
    second_ref, third_ref, table_ref = refs[NY + 3 :]
    y = lax.axis_index("y")
    fill_own(packed, table_ref)
    for i, s in enumerate(STEPS):
        table_ref[lax.rem(y + NY - s, NY) + NY] = other_ref[i].astype(f32)
    count = second_ref.shape[1]
    both = ((0, hidden_ref), (1, across_ref))
    send_rows(capacity, table_ref, both, count, second_ref)
    send_rows(capacity, table_ref, both[1:], 2 * count, third_ref)


def up_kernel(width, *refs):
    pieces, (gain_ref, gate_ref, lift_ref, out_ref) = refs[:NX], refs[NX:]
    x = lax.axis_index("x")
    squares = None
    for ref in pieces:
        h = ref[...].astype(f32)
        s = jnp.sum(h * h, axis=1, keepdims=True)
        squares = s if squares is None else squares + s
    scale = lax.rsqrt(squares * (1.0 / width) + epsilon)
    gate = lift = None
    for ref, back in zip(pieces, STEPS):
        q = lax.rem(x + NX - back, NX)
        normed = (ref[...].astype(f32) * scale * gain_ref[pl.ds(q, 1), :]).astype(bf16)
        g = jnp.dot(normed, gate_ref[q], preferred_element_type=f32)
        l = jnp.dot(normed, lift_ref[q], preferred_element_type=f32)
        gate = g if gate is None else gate + g
        lift = l if lift is None else lift + l
    out_ref[...] = (gate / (1.0 + jnp.exp(-gate)) * lift).astype(bf16)


def down_kernel(*refs):
    acts, downs, out_ref = refs[:NX], refs[NX : 2 * NX], refs[2 * NX]
    total = None
    for act, down in zip(acts, downs):
        part = jnp.dot(act[...], down[...], preferred_element_type=f32)
        part = part.astype(bf16).astype(f32)
        total = part if total is None else total + part
    out_ref[...] = total.astype(bf16)


def combine_kernel(capacity, start, begin, table_ref, rows_ref, *refs):
    rest, out_ref = refs[:-1], refs[-1]
    tokens = table_ref.shape[2]
    block = pl.program_id(0) + start
    first = block * capacity - begin
    at = jnp.clip(first, 0, rows_ref.shape[1] - 32) // 16 * 16
    window = pl.ds(pl.multiple_of(at, 16), 32)
    slots = lax.broadcasted_iota(jnp.int32, (32, tokens), 0) + (at - first)
    slots = slots.astype(f32)
    spread, rows = [], []
    for d in range(NZ):
        hit = (slots == table_ref[0, d : d + 1, :]) & (slots >= 0.0)
        for part in (1, 2):
            gate = table_ref[0, part * NZ + d : part * NZ + d + 1, :]
            spread.append(jnp.where(hit, gate, 0.0))
            rows.append(rows_ref[d, window, :])
    total = lax.dot_general(
        jnp.concatenate(spread, axis=0).astype(bf16),
        jnp.concatenate(rows, axis=0),
        BY_ROWS,
        preferred_element_type=f32,
    )
    if rest:
        total = total + rest[0][0]
    out_ref[0] = total.astype(out_ref.dtype)


def merge_kernel(own_ref, got_ref, *outs):
    y = lax.axis_index("y")
    for s, out_ref in zip(STEPS, outs):
        there = lax.rem(y + s, NY)
        out_ref[...] = (own_ref[there] + got_ref[there].astype(f32)).astype(out_ref.dtype)


def final_kernel(hidden_ref, *refs):
    total = refs[0][...]
    for ref in refs[1:-1]:
        total = total + ref[...].astype(f32)
    refs[-1][...] = (hidden_ref[...].astype(f32) + total).astype(bf16)


def body(
    context,
    residual_in,
    out_weight,
    norm_gain,
    expert_ids,
    gate_weights,
    gate_matrix,
    lift_matrix,
    down_matrix,
):
    tokens, width = residual_in.shape
    top = expert_ids.shape[1]
    share = width // NX
    fine = share // NY
    units = gate_matrix.shape[2]
    capacity = min(tokens, max(2, tokens * top * 9 // (8 * NE)))
    blocks = NY * NC
    slots = blocks * capacity
    x = lax.axis_index("x")

    contexts = [shift(context, "y", NY, s) for s in STEPS]
    weight = jnp.concatenate(z_ring(out_weight.T), axis=0)
    weight, contexts = lax.optimization_barrier((weight, contexts))
    packed = call(
        route_kernel,
        "route",
        [shape(tokens + TABLE, fine)] * NY,
        expert_ids.T,
        gate_weights.T,
        residual_in,
    )
    parts = call(
        project_kernel,
        "project",
        [shape(NY, tokens, fine, dtype=f32)] + [shape(NY, tokens, fine)] * (NX - 1),
        *contexts,
        weight,
        swap(weight),
        scratch=[pltpu.VMEM((NZ, NC * weight.shape[0] // NZ, share), bf16)],
        flops=2 * NY * tokens * share * width // NY,
    )
    parts, packed = lax.optimization_barrier((parts, packed))
    parts = x_exchange(parts)
    packed = y_exchange(packed)
    table = swap(call(pick_kernel, "pick", shape(NY, TABLE, tokens), *packed))
    parts, table = lax.optimization_barrier((parts, table))
    hidden = call(hidden_kernel, "hidden", shape(NY * tokens, fine), *parts, *packed)
    hidden, down_here = lax.optimization_barrier((hidden, down_matrix[0]))
    pieces = [shift(hidden, "y", NY, s) for s in STEPS]
    downs = x_exchange(
        [
            lax.dynamic_slice_in_dim(down_here, lax.rem(x + s, NX) * share, share, 1)
            for s in STEPS
        ]
    )
    hidden = call(gather_kernel, "gather", shape(NY * tokens, share), *pieces)
    count = slots // CHUNKS
    sent0, own = call(
        functools.partial(dispatch_own_kernel, capacity),
        "dispatch_own",
        [shape(NZ, count, share), shape(tokens, share)],
        *packed,
        hidden,
        scratch=[pltpu.VMEM((NY, TABLE, tokens), f32)],
        flops=2 * NZ * count * NY * tokens * share,
    )
    got0 = z_exchange(sent0)
    across, own = lax.optimization_barrier((swap(hidden), own))
    sent1, sent2, table = call(
        functools.partial(dispatch_kernel, capacity),
        "dispatch",
        [shape(NZ, count, share)] * 2 + [shape(blocks, TABLE, tokens, dtype=f32)],
        *packed,
        table,
        hidden,
        across,
        flops=6 * NZ * count * NY * tokens * share,
    )

    gain = norm_gain.astype(f32).reshape(NX, share)
    gate_here = gate_matrix.reshape(NX, share, units)
    lift_here = lift_matrix.reshape(NX, share, units)
    rows_here = NZ * count
    got0, sent1, downs = lax.optimization_barrier((got0, sent1, downs))
    got1 = z_exchange(sent1)
    ring0 = x_ring(got0.reshape(rows_here, share), 0)
    got1, sent2, *two = lax.optimization_barrier((got1, sent2, *ring0[1:3]))
    ring0 = ring0[0], *two, ring0[3]
    got2 = z_exchange(sent2)
    acts = []
    for i, rows in enumerate((got0, got1, got2)):
        if i == 2:
            rows, acts[0] = lax.optimization_barrier((rows, acts[0]))
            got2 = rows
        rows = rows.reshape(rows_here, share)
        acts.append(
            call(
                functools.partial(up_kernel, width),
                f"up{i}",
                shape(rows_here, units),
                *(x_ring(rows, i) if i else ring0),
                gain,
                gate_here,
                lift_here,
                flops=4 * rows_here * width * units,
            )
        )
    lists = []
    for i, act in enumerate(acts):
        back = call(
            down_kernel,
            f"down{i}",
            shape(rows_here, share),
            *x_ring(act, i),
            *downs,
            flops=2 * rows_here * NX * units * share,
            grid=(share // 256,),
            specs=(
                [pl.BlockSpec((rows_here, units), lambda i: (0, 0))] * NX
                + [pl.BlockSpec((units, 256), lambda i: (0, i))] * NX,
                pl.BlockSpec((rows_here, 256), lambda i: (0, i)),
            ),
        )
        back, last = lax.optimization_barrier((back, lists[-1] if lists else got2))
        if lists:
            lists[-1] = last
        lists.append(z_exchange(back.reshape(NZ, count, share)))

    def combine(i, start, dtype, total=None):
        part = pl.BlockSpec((1, tokens, share), lambda b: (b, 0, 0))
        rest = [] if total is None else [total]
        return call(
            functools.partial(combine_kernel, capacity, start, i * count),
            f"combine{i}_{start}",
            shape(NY, tokens, share, dtype=dtype),
            table,
            lists[i],
            *rest,
            flops=4 * NZ * NY * 32 * tokens * share,
            grid=(NY,),
            specs=(
                [
                    pl.BlockSpec((1, TABLE, tokens), lambda b: (b + start, 0, 0)),
                    pl.BlockSpec((NZ, count, share), lambda b: (0, 0, 0)),
                ]
                + [part] * len(rest),
                part,
            ),
        )

    mine = combine(1, 0, f32, combine(0, 0, f32))
    crossing = combine(2, NY, bf16, combine(1, NY, f32))
    merged = call(
        merge_kernel,
        "merge",
        [shape(tokens, share, dtype=f32)] + [shape(tokens, share)] * (NY - 1),
        mine,
        swap(crossing),
    )
    return call(final_kernel, "final", shape(tokens, share), own, *y_exchange(merged))


def solution(mesh):
    fine = Mesh(mesh.devices.reshape(NZ, NY, NC, NX), ("z", "y", "c", "x"))
    e = ("z", "y", "c")
    placed = (
        P(e, "x"),
        P(e, None),
        P("x", e),
        P(),
        P(e, None),
        P(e, None),
        P(e, None, "x"),
        P(e, None, "x"),
        P(e, "x", None),
    )
    return jax.shard_map(body, mesh=fine, in_specs=placed, out_specs=P(e, "x"), check_vma=False)
```

```python
import functools

import jax
import jax.numpy as jnp
from jax import lax
from jax.experimental import pallas as pl
from jax.experimental.pallas import tpu as pltpu
from jax.sharding import Mesh
from jax.sharding import PartitionSpec as P

epsilon = 1e-06
f32 = jnp.float32
bf16 = jnp.bfloat16
NZ, NY, NC, NX = 8, 4, 2, 4
NE = NZ * NY * NC
STEPS = (0, 1, 3, 2)
GROUPS = ((0, 1, -1), (4,), (3, -3), (2, -2))
SHIFTS = sum(GROUPS, ())
RING = (0, 1, -1, 2, -2, 3, -3)
TABLE = 32
BY_ROWS = (((0,), (0,)), ((), ()))
BY_COLUMNS = (((1,), (1,)), ((), ()))


def shape(*dims, dtype=bf16):
    return jax.ShapeDtypeStruct(dims, dtype)


def call(kernel, name, outs, *args, scratch=(), mib=40, flops=0, grid=(), specs=None):
    size = sum(a.size * a.dtype.itemsize for a in args)
    blocks = {} if specs is None else dict(grid=grid, in_specs=specs[0], out_specs=specs[1])
    return pl.pallas_call(
        kernel,
        out_shape=outs,
        scratch_shapes=scratch,
        **blocks,
        compiler_params=pltpu.CompilerParams(vmem_limit_bytes=mib << 20),
        cost_estimate=pl.CostEstimate(flops=flops, bytes_accessed=size, transcendentals=0),
        name=name,
    )(*args)


def shift(value, axis, count, step):
    if step % count == 0:
        return value
    return lax.ppermute(value, axis, [(i, (i + step) % count) for i in range(count)])


def y_exchange(values):
    return [shift(v, "y", NY, s) for v, s in zip(values, STEPS)]


def x_exchange(values):
    return [shift(v, "x", NX, s) for v, s in zip(values, STEPS)]


def swap(value):
    return shift(value, "c", NC, 1)


def x_ring(value, way):
    right, left = shift(value, "x", NX, 1), shift(value, "x", NX, -1)
    right, left = lax.optimization_barrier((right, left))
    far = shift(right, "x", NX, 1) if way else shift(left, "x", NX, -1)
    return value, right, left, far


def z_ring(value):
    right = left = value
    pieces = [value]
    for _ in range(NZ // 2 - 1):
        right, left = shift(right, "z", NZ, 1), shift(left, "z", NZ, -1)
        pieces += [right, left]
    half = value.shape[0] // 2
    return pieces + [shift(right[:half], "z", NZ, 1), shift(left[half:], "z", NZ, -1)]


def route_kernel(ids_ref, gates_ref, residual_ref, *outs):
    tokens = ids_ref.shape[1]
    x, y = lax.axis_index("x"), lax.axis_index("y")
    row = lax.broadcasted_iota(jnp.int32, (NE, tokens), 0)
    group = row // (NC * NZ)
    step = group ^ (group >> 1)
    experts = (row % NZ) * (NY * NC) + ((y + step) % NY) * NC + (row // NZ) % NC
    chosen = jnp.zeros((NE, tokens), f32)
    weight = jnp.zeros((NE, tokens), f32)
    for k in range(ids_ref.shape[0]):
        same = experts == ids_ref[k : k + 1, :]
        chosen = jnp.where(same, 1.0, chosen)
        weight = jnp.where(same, gates_ref[k : k + 1, :], weight)
    rows = lax.broadcasted_iota(jnp.int32, (tokens, tokens), 0)
    columns = lax.broadcasted_iota(jnp.int32, (tokens, tokens), 1)
    before = jnp.where(rows < columns, 1.0, 0.0).astype(bf16)
    rank = jnp.dot(chosen.astype(bf16), before, preferred_element_type=f32)
    slot = jnp.where(chosen > 0.0, rank, -1.0)
    high = weight.astype(bf16).astype(f32)
    low = weight - high
    share = residual_ref.shape[1] // NX
    half, piece = share // 2, share // 8
    for i, (s, out_ref) in enumerate(zip(STEPS, outs)):
        there = lax.rem(y + s, NY)
        for b in range(2):
            column = pl.multiple_of(x * share + b * half + there * piece, piece)
            out_ref[:tokens, b * piece : (b + 1) * piece] = residual_ref[:, pl.ds(column, piece)]
        for c in range(NC):
            at = (i * NC + c) * NZ
            part = [t[at : at + NZ] for t in (slot, high, low)]
            part.append(jnp.zeros((NZ, tokens), f32))
            part = jnp.concatenate(part, axis=0).astype(bf16)
            out_ref[tokens:, c * tokens : (c + 1) * tokens] = part


def project_kernel(*refs):
    contexts, (mine_ref, other_ref), outs = refs[:NY], refs[NY : NY + 2], refs[NY + 2 : -1]
    all_ref = refs[-1]
    width = all_ref.shape[1] // NC
    x, z, c = lax.axis_index("x"), lax.axis_index("z"), lax.axis_index("c")
    for i in range(NZ):
        owner = lax.rem(z + NZ - (RING + (4,))[i], NZ)
        for ref, core in ((mine_ref, c), (other_ref, 1 - c)):
            there = pl.ds(pl.multiple_of(core * width, width), width)
            all_ref[owner, there, :] = ref[i * width : (i + 1) * width, :]
    for step, out_ref in zip(STEPS, outs):
        q = lax.rem(x + step, NX)
        weight = all_ref[pl.ds(2 * q, 2)].reshape(out_ref.shape[2], -1)
        for i, ref in enumerate(contexts):
            part = lax.dot_general(ref[...], weight, BY_COLUMNS, preferred_element_type=f32)
            out_ref[i] = part.astype(out_ref.dtype)


def hidden_kernel(*refs):
    parts, packed, out_ref = refs[:NX], refs[NX : NX + NY], refs[NX + NY]
    tokens = parts[0].shape[1]
    y = lax.axis_index("y")
    for i, s in enumerate(STEPS):
        total = parts[0][i]
        for ref in parts[1:]:
            total = total + ref[i].astype(f32)
        owner = lax.rem(y + NY - s, NY)
        residual = packed[i][:tokens, :].astype(f32)
        out_ref[pl.ds(pl.multiple_of(owner * tokens, tokens), tokens), :] = (
            residual + total
        ).astype(bf16)


def fill_table(packed, other_ref, table_ref):
    tokens = table_ref.shape[2]
    y, c = lax.axis_index("y"), lax.axis_index("c")
    mine = pl.ds(pl.multiple_of(c * tokens, tokens), tokens)
    for i, s in enumerate(STEPS):
        owner = lax.rem(y + NY - s, NY)
        table_ref[owner] = packed[i][-TABLE:, mine].astype(f32)
        table_ref[owner + NY] = other_ref[i].astype(f32)


def pick_kernel(*refs):
    packed, out_ref = refs[:NY], refs[NY]
    tokens = out_ref.shape[2]
    c = lax.axis_index("c")
    others = pl.ds(pl.multiple_of((1 - c) * tokens, tokens), tokens)
    for i in range(NY):
        out_ref[i] = packed[i][-TABLE:, others]


def gather_kernel(*refs):
    pieces, out_ref = refs[:NY], refs[NY]
    y = lax.axis_index("y")
    piece = pieces[0].shape[1] // 2
    half = out_ref.shape[1] // 2
    for ref, s in zip(pieces, STEPS):
        owner = lax.rem(y + NY - s, NY)
        for b in range(2):
            column = pl.multiple_of(b * half + owner * piece, piece)
            out_ref[:, pl.ds(column, piece)] = ref[:, b * piece : (b + 1) * piece]


def dispatch_kernel(capacity, *refs):
    packed, other_ref = refs[:NY], refs[NY]
    hidden_ref, across_ref = refs[NY + 1 : NY + 3]
    sent, (own_ref, table_out, table_ref) = refs[NY + 3 : -3], refs[-3:]
    tokens = own_ref.shape[0]
    blocks = NY * NC
    y, z = lax.axis_index("y"), lax.axis_index("z")
    fill_table(packed, other_ref, table_ref)
    table_out[...] = table_ref[...]
    own_ref[...] = hidden_ref[pl.ds(pl.multiple_of(y * tokens, tokens), tokens), :]
    slots = lax.broadcasted_iota(jnp.int32, (blocks * capacity, NY * tokens), 0)
    for s, out_ref in zip(SHIFTS, sent):
        d = lax.rem(z + NZ + s, NZ)
        rows = None
        for core, ref in enumerate((hidden_ref, across_ref)):
            parts = []
            for b in range(core * NY, core * NY + NY):
                slot = table_ref[b, pl.ds(d, 1), :]
                parts.append(jnp.where(slot >= 0.0, slot + float(b * capacity), -1.0))
            place = jnp.concatenate(parts, axis=1).astype(jnp.int32)
            pick = jnp.where(slots == place, 1.0, 0.0).astype(bf16)
            part = jnp.dot(pick, ref[...], preferred_element_type=f32)
            rows = part if rows is None else rows + part
        out_ref[...] = rows.astype(bf16)


def up_kernel(width, *refs):
    pieces, (gain_ref, gate_ref, lift_ref, out_ref) = refs[:NX], refs[NX:]
    x = lax.axis_index("x")
    squares = None
    for ref in pieces:
        h = ref[...].astype(f32)
        s = jnp.sum(h * h, axis=1, keepdims=True)
        squares = s if squares is None else squares + s
    scale = lax.rsqrt(squares * (1.0 / width) + epsilon)
    gate = lift = None
    for ref, back in zip(pieces, STEPS):
        q = lax.rem(x + NX - back, NX)
        normed = (ref[...].astype(f32) * scale * gain_ref[pl.ds(q, 1), :]).astype(bf16)
        g = jnp.dot(normed, gate_ref[q], preferred_element_type=f32)
        l = jnp.dot(normed, lift_ref[q], preferred_element_type=f32)
        gate = g if gate is None else gate + g
        lift = l if lift is None else lift + l
    out_ref[...] = (gate / (1.0 + jnp.exp(-gate)) * lift).astype(bf16)


def down_kernel(*refs):
    acts, downs, outs = refs[:NX], refs[NX : 2 * NX], refs[2 * NX :]
    total = None
    for act, down in zip(acts, downs):
        part = jnp.dot(act[...], down[...], preferred_element_type=f32)
        part = part.astype(bf16).astype(f32)
        total = part if total is None else total + part
    total = total.astype(bf16)
    rows = outs[0].shape[0]
    for i, out in enumerate(outs):
        out[...] = total[i * rows : (i + 1) * rows]


def combine_kernel(capacity, start, shifts, table_ref, *refs):
    lists, rest, out_ref = refs[: len(shifts)], refs[len(shifts) : -1], refs[-1]
    tokens = table_ref.shape[2]
    block = pl.program_id(0) + start
    z = lax.axis_index("z")
    first = (block * capacity) // 16 * 16
    window = pl.ds(pl.multiple_of(first, 16), 32)
    slots = lax.broadcasted_iota(jnp.int32, (32, tokens), 0) - (block * capacity - first)
    slots = slots.astype(f32)
    spread, rows = [], []
    for s, ref in zip(shifts, lists):
        d = lax.rem(z + NZ + s, NZ)
        hit = (slots == table_ref[0, pl.ds(d, 1), :]) & (slots >= 0.0)
        for part in (1, 2):
            gate = table_ref[0, pl.ds(part * NZ + d, 1), :]
            spread.append(jnp.where(hit, gate, 0.0))
            rows.append(ref[window, :])
    total = lax.dot_general(
        jnp.concatenate(spread, axis=0).astype(bf16),
        jnp.concatenate(rows, axis=0),
        BY_ROWS,
        preferred_element_type=f32,
    )
    if rest:
        total = total + rest[0][0]
    out_ref[0] = total.astype(out_ref.dtype)


def merge_kernel(own_ref, got_ref, *outs):
    y = lax.axis_index("y")
    for s, out_ref in zip(STEPS, outs):
        there = lax.rem(y + s, NY)
        out_ref[...] = (own_ref[there] + got_ref[there].astype(f32)).astype(out_ref.dtype)


def final_kernel(hidden_ref, *refs):
    total = refs[0][...]
    for ref in refs[1:-1]:
        total = total + ref[...].astype(f32)
    refs[-1][...] = (hidden_ref[...].astype(f32) + total).astype(bf16)


def body(
    context,
    residual_in,
    out_weight,
    norm_gain,
    expert_ids,
    gate_weights,
    gate_matrix,
    lift_matrix,
    down_matrix,
):
    tokens, width = residual_in.shape
    top = expert_ids.shape[1]
    share = width // NX
    fine = share // NY
    units = gate_matrix.shape[2]
    capacity = min(tokens, max(2, tokens * top * 9 // (8 * NE)))
    blocks = NY * NC
    slots = blocks * capacity
    x = lax.axis_index("x")

    contexts = [shift(context, "y", NY, s) for s in STEPS]
    weight = jnp.concatenate(z_ring(out_weight.T), axis=0)
    packed = call(
        route_kernel,
        "route",
        [shape(tokens + TABLE, fine)] * NY,
        expert_ids.T,
        gate_weights.T,
        residual_in,
    )
    packed = y_exchange(packed)
    table = swap(call(pick_kernel, "pick", shape(NY, TABLE, tokens), *packed))
    down_here, *contexts = lax.optimization_barrier((down_matrix[0], *contexts))
    downs = [
        lax.dynamic_slice_in_dim(down_here, lax.rem(x + s, NX) * share, share, 1) for s in STEPS
    ]
    weight, contexts, downs = lax.optimization_barrier((weight, contexts, downs))
    across, table = lax.optimization_barrier((swap(weight), table))
    parts = call(
        project_kernel,
        "project",
        [shape(NY, tokens, fine, dtype=f32)] + [shape(NY, tokens, fine)] * (NX - 1),
        *contexts,
        weight,
        across,
        scratch=[pltpu.VMEM((NZ, NC * weight.shape[0] // NZ, share), bf16)],
        flops=2 * NY * tokens * share * width // NY,
    )
    parts = x_exchange(parts)
    parts, downs = lax.optimization_barrier((parts, downs))
    downs = x_exchange(downs)
    hidden = call(hidden_kernel, "hidden", shape(NY * tokens, fine), *parts, *packed)
    pieces = [shift(hidden, "y", NY, s) for s in STEPS]
    pieces, downs[1:3] = lax.optimization_barrier((pieces, downs[1:3]))
    hidden = call(gather_kernel, "gather", shape(NY * tokens, share), *pieces)
    *sent, own, table = call(
        functools.partial(dispatch_kernel, capacity),
        "dispatch",
        [shape(slots, share)] * NZ
        + [shape(tokens, share), shape(blocks, TABLE, tokens, dtype=f32)],
        *packed,
        table,
        hidden,
        swap(hidden),
        scratch=[pltpu.VMEM((blocks, TABLE, tokens), f32)],
        flops=2 * NZ * slots * blocks * tokens * share,
    )

    gain = norm_gain.astype(f32).reshape(NX, share)
    gate_here = gate_matrix.reshape(NX, share, units)
    lift_here = lift_matrix.reshape(NX, share, units)

    sent = dict(zip(SHIFTS, sent))
    got, acts = [], []
    before = None
    for group in GROUPS:
        rows = [sent[s] for s in group]
        if before is not None:
            *rows, got[-1] = lax.optimization_barrier((*rows, got[-1]))
        before = group
        rows = [shift(r, "z", NZ, s) for r, s in zip(rows, group)]
        if not got:
            *rows, downs[3] = lax.optimization_barrier((*rows, downs[3]))
        got.append(rows[0] if len(rows) == 1 else jnp.concatenate(rows, axis=0))
    for i, group in enumerate(GROUPS):
        rows = got[i]
        if i >= 2:
            rows, acts[i - 2] = lax.optimization_barrier((rows, acts[i - 2]))
        count = rows.shape[0]
        ring = x_ring(rows, i < 2)
        acts.append(
            call(
                functools.partial(up_kernel, width),
                f"up{i}",
                shape(count, units),
                *ring,
                gain,
                gate_here,
                lift_here,
                flops=4 * count * width * units,
            )
        )
    total = None
    for i, group in enumerate(GROUPS):
        count = got[i].shape[0]
        back = call(
            down_kernel,
            f"down{i}",
            [shape(slots, share)] * len(group),
            *x_ring(acts[i], i < 2),
            *downs,
            flops=2 * count * NX * units * share,
            grid=(share // 256,),
            specs=(
                [pl.BlockSpec((count, units), lambda i: (0, 0))] * NX
                + [pl.BlockSpec((units, 256), lambda i: (0, i))] * NX,
                [pl.BlockSpec((slots, 256), lambda i: (0, i))] * len(group),
            ),
        )
        lists = [shift(r, "z", NZ, -s) for r, s in zip(back, group)]

        def combine(start, number, dtype, total=total, lists=lists, group=group, i=i):
            part = pl.BlockSpec((1, tokens, share), lambda b: (b, 0, 0))
            there = pl.BlockSpec((1, tokens, share), lambda b: (b + start, 0, 0))
            return call(
                functools.partial(combine_kernel, capacity, start, group),
                f"combine{i}_{start}",
                shape(number, tokens, share, dtype=dtype),
                table,
                *lists,
                *([] if total is None else [total]),
                flops=4 * len(group) * number * 32 * tokens * share,
                grid=(number,),
                specs=(
                    [pl.BlockSpec((1, TABLE, tokens), lambda b: (b + start, 0, 0))]
                    + [pl.BlockSpec((slots, share), lambda b: (0, 0))] * len(group)
                    + ([] if total is None else [there]),
                    part,
                ),
            )

        if i < len(GROUPS) - 1:
            total = combine(0, blocks, f32)
    crossing = combine(NY, NY, bf16)
    mine = combine(0, NY, f32)
    merged = call(
        merge_kernel,
        "merge",
        [shape(tokens, share, dtype=f32)] + [shape(tokens, share)] * (NY - 1),
        mine,
        swap(crossing),
    )
    return call(final_kernel, "final", shape(tokens, share), own, *y_exchange(merged))


def solution(mesh):
    fine = Mesh(mesh.devices.reshape(NZ, NY, NC, NX), ("z", "y", "c", "x"))
    e = ("z", "y", "c")
    placed = (
        P(e, "x"),
        P(e, None),
        P("x", e),
        P(),
        P(e, None),
        P(e, None),
        P(e, None, "x"),
        P(e, None, "x"),
        P(e, "x", None),
    )
    return jax.shard_map(body, mesh=fine, in_specs=placed, out_specs=P(e, "x"), check_vma=False)
```

```python
import functools

import jax
import jax.numpy as jnp
from jax import lax
from jax.experimental import pallas as pl
from jax.experimental.pallas import tpu as pltpu
from jax.sharding import Mesh
from jax.sharding import PartitionSpec as P

epsilon = 1e-06
f32 = jnp.float32
bf16 = jnp.bfloat16
NZ, NY, NC, NX = 8, 4, 2, 4
NE = NZ * NY * NC
STEPS = (0, 1, 3, 2)
GROUPS = ((0, 1, -1), (4,), (3, -3), (2, -2))
SHIFTS = sum(GROUPS, ())
RING = (0, 1, -1, 2, -2, 3, -3)
TABLE = 32
BY_ROWS = (((0,), (0,)), ((), ()))
BY_COLUMNS = (((1,), (1,)), ((), ()))


def shape(*dims, dtype=bf16):
    return jax.ShapeDtypeStruct(dims, dtype)


def call(kernel, name, outs, *args, scratch=(), mib=40, flops=0, grid=(), specs=None):
    size = sum(a.size * a.dtype.itemsize for a in args)
    blocks = {} if specs is None else dict(grid=grid, in_specs=specs[0], out_specs=specs[1])
    return pl.pallas_call(
        kernel,
        out_shape=outs,
        scratch_shapes=scratch,
        **blocks,
        compiler_params=pltpu.CompilerParams(vmem_limit_bytes=mib << 20),
        cost_estimate=pl.CostEstimate(flops=flops, bytes_accessed=size, transcendentals=0),
        name=name,
    )(*args)


def shift(value, axis, count, step):
    if step % count == 0:
        return value
    return lax.ppermute(value, axis, [(i, (i + step) % count) for i in range(count)])


def y_exchange(values):
    return [shift(v, "y", NY, s) for v, s in zip(values, STEPS)]


def x_exchange(values):
    return [shift(v, "x", NX, s) for v, s in zip(values, STEPS)]


def swap(value):
    return shift(value, "c", NC, 1)


def x_ring(value, way):
    right, left = shift(value, "x", NX, 1), shift(value, "x", NX, -1)
    right, left = lax.optimization_barrier((right, left))
    far = shift(right, "x", NX, 1) if way else shift(left, "x", NX, -1)
    return value, right, left, far


def z_ring(value):
    right = left = value
    pieces = [value]
    for _ in range(NZ // 2 - 1):
        right, left = shift(right, "z", NZ, 1), shift(left, "z", NZ, -1)
        pieces += [right, left]
    half = value.shape[0] // 2
    return pieces + [shift(right[:half], "z", NZ, 1), shift(left[half:], "z", NZ, -1)]


def route_kernel(ids_ref, gates_ref, residual_ref, *outs):
    tokens = ids_ref.shape[1]
    x, y = lax.axis_index("x"), lax.axis_index("y")
    row = lax.broadcasted_iota(jnp.int32, (NE, tokens), 0)
    group = row // (NC * NZ)
    step = group ^ (group >> 1)
    experts = (row % NZ) * (NY * NC) + ((y + step) % NY) * NC + (row // NZ) % NC
    chosen = jnp.zeros((NE, tokens), f32)
    weight = jnp.zeros((NE, tokens), f32)
    for k in range(ids_ref.shape[0]):
        same = experts == ids_ref[k : k + 1, :]
        chosen = jnp.where(same, 1.0, chosen)
        weight = jnp.where(same, gates_ref[k : k + 1, :], weight)
    rows = lax.broadcasted_iota(jnp.int32, (tokens, tokens), 0)
    columns = lax.broadcasted_iota(jnp.int32, (tokens, tokens), 1)
    before = jnp.where(rows < columns, 1.0, 0.0).astype(bf16)
    rank = jnp.dot(chosen.astype(bf16), before, preferred_element_type=f32)
    slot = jnp.where(chosen > 0.0, rank, -1.0)
    high = weight.astype(bf16).astype(f32)
    low = weight - high
    share = residual_ref.shape[1] // NX
    half, piece = share // 2, share // 8
    for i, (s, out_ref) in enumerate(zip(STEPS, outs)):
        there = lax.rem(y + s, NY)
        for b in range(2):
            column = pl.multiple_of(x * share + b * half + there * piece, piece)
            out_ref[:tokens, b * piece : (b + 1) * piece] = residual_ref[:, pl.ds(column, piece)]
        for c in range(NC):
            at = (i * NC + c) * NZ
            part = [t[at : at + NZ] for t in (slot, high, low)]
            part.append(jnp.zeros((NZ, tokens), f32))
            part = jnp.concatenate(part, axis=0).astype(bf16)
            out_ref[tokens:, c * tokens : (c + 1) * tokens] = part


def project_kernel(*refs):
    contexts, (mine_ref, other_ref), outs = refs[:NY], refs[NY : NY + 2], refs[NY + 2 : -1]
    all_ref = refs[-1]
    width = all_ref.shape[1] // NC
    x, z, c = lax.axis_index("x"), lax.axis_index("z"), lax.axis_index("c")
    for i in range(NZ):
        owner = lax.rem(z + NZ - (RING + (4,))[i], NZ)
        for ref, core in ((mine_ref, c), (other_ref, 1 - c)):
            there = pl.ds(pl.multiple_of(core * width, width), width)
            all_ref[owner, there, :] = ref[i * width : (i + 1) * width, :]
    for step, out_ref in zip(STEPS, outs):
        q = lax.rem(x + step, NX)
        weight = all_ref[pl.ds(2 * q, 2)].reshape(out_ref.shape[2], -1)
        for i, ref in enumerate(contexts):
            part = lax.dot_general(ref[...], weight, BY_COLUMNS, preferred_element_type=f32)
            out_ref[i] = part.astype(out_ref.dtype)


def hidden_kernel(*refs):
    parts, packed, out_ref = refs[:NX], refs[NX : NX + NY], refs[NX + NY]
    tokens = parts[0].shape[1]
    y = lax.axis_index("y")
    for i, s in enumerate(STEPS):
        total = parts[0][i]
        for ref in parts[1:]:
            total = total + ref[i].astype(f32)
        owner = lax.rem(y + NY - s, NY)
        residual = packed[i][:tokens, :].astype(f32)
        out_ref[pl.ds(pl.multiple_of(owner * tokens, tokens), tokens), :] = (
            residual + total
        ).astype(bf16)


def fill_table(packed, other_ref, table_ref):
    tokens = table_ref.shape[2]
    y, c = lax.axis_index("y"), lax.axis_index("c")
    mine = pl.ds(pl.multiple_of(c * tokens, tokens), tokens)
    for i, s in enumerate(STEPS):
        owner = lax.rem(y + NY - s, NY)
        table_ref[owner] = packed[i][-TABLE:, mine].astype(f32)
        table_ref[owner + NY] = other_ref[i].astype(f32)


def pick_kernel(*refs):
    packed, out_ref = refs[:NY], refs[NY]
    tokens = out_ref.shape[2]
    c = lax.axis_index("c")
    others = pl.ds(pl.multiple_of((1 - c) * tokens, tokens), tokens)
    for i in range(NY):
        out_ref[i] = packed[i][-TABLE:, others]


def gather_kernel(*refs):
    pieces, out_ref = refs[:NY], refs[NY]
    y = lax.axis_index("y")
    piece = pieces[0].shape[1] // 2
    half = out_ref.shape[1] // 2
    for ref, s in zip(pieces, STEPS):
        owner = lax.rem(y + NY - s, NY)
        for b in range(2):
            column = pl.multiple_of(b * half + owner * piece, piece)
            out_ref[:, pl.ds(column, piece)] = ref[:, b * piece : (b + 1) * piece]


def dispatch_kernel(capacity, *refs):
    packed, other_ref = refs[:NY], refs[NY]
    hidden_ref, across_ref = refs[NY + 1 : NY + 3]
    sent, (own_ref, table_out, table_ref) = refs[NY + 3 : -3], refs[-3:]
    tokens = own_ref.shape[0]
    blocks = NY * NC
    y, z = lax.axis_index("y"), lax.axis_index("z")
    fill_table(packed, other_ref, table_ref)
    table_out[...] = table_ref[...]
    own_ref[...] = hidden_ref[pl.ds(pl.multiple_of(y * tokens, tokens), tokens), :]
    slots = lax.broadcasted_iota(jnp.int32, (blocks * capacity, NY * tokens), 0)
    for s, out_ref in zip(SHIFTS, sent):
        d = lax.rem(z + NZ + s, NZ)
        rows = None
        for core, ref in enumerate((hidden_ref, across_ref)):
            parts = []
            for b in range(core * NY, core * NY + NY):
                slot = table_ref[b, pl.ds(d, 1), :]
                parts.append(jnp.where(slot >= 0.0, slot + float(b * capacity), -1.0))
            place = jnp.concatenate(parts, axis=1).astype(jnp.int32)
            pick = jnp.where(slots == place, 1.0, 0.0).astype(bf16)
            part = jnp.dot(pick, ref[...], preferred_element_type=f32)
            rows = part if rows is None else rows + part
        out_ref[...] = rows.astype(bf16)


def up_kernel(width, *refs):
    pieces, (gain_ref, gate_ref, lift_ref, out_ref) = refs[:NX], refs[NX:]
    x = lax.axis_index("x")
    squares = None
    for ref in pieces:
        h = ref[...].astype(f32)
        s = jnp.sum(h * h, axis=1, keepdims=True)
        squares = s if squares is None else squares + s
    scale = lax.rsqrt(squares * (1.0 / width) + epsilon)
    gate = lift = None
    for ref, back in zip(pieces, STEPS):
        q = lax.rem(x + NX - back, NX)
        normed = (ref[...].astype(f32) * scale * gain_ref[pl.ds(q, 1), :]).astype(bf16)
        g = jnp.dot(normed, gate_ref[q], preferred_element_type=f32)
        l = jnp.dot(normed, lift_ref[q], preferred_element_type=f32)
        gate = g if gate is None else gate + g
        lift = l if lift is None else lift + l
    out_ref[...] = (gate / (1.0 + jnp.exp(-gate)) * lift).astype(bf16)


def down_kernel(*refs):
    acts, downs, outs = refs[:NX], refs[NX : 2 * NX], refs[2 * NX :]
    total = None
    for act, down in zip(acts, downs):
        part = jnp.dot(act[...], down[...], preferred_element_type=f32)
        part = part.astype(bf16).astype(f32)
        total = part if total is None else total + part
    total = total.astype(bf16)
    rows = outs[0].shape[0]
    for i, out in enumerate(outs):
        out[...] = total[i * rows : (i + 1) * rows]


def combine_kernel(capacity, start, shifts, table_ref, *refs):
    lists, rest, out_ref = refs[: len(shifts)], refs[len(shifts) : -1], refs[-1]
    tokens = table_ref.shape[2]
    block = pl.program_id(0) + start
    z = lax.axis_index("z")
    first = (block * capacity) // 16 * 16
    window = pl.ds(pl.multiple_of(first, 16), 32)
    slots = lax.broadcasted_iota(jnp.int32, (32, tokens), 0) - (block * capacity - first)
    slots = slots.astype(f32)
    spread, rows = [], []
    for s, ref in zip(shifts, lists):
        d = lax.rem(z + NZ + s, NZ)
        hit = (slots == table_ref[0, pl.ds(d, 1), :]) & (slots >= 0.0)
        for part in (1, 2):
            gate = table_ref[0, pl.ds(part * NZ + d, 1), :]
            spread.append(jnp.where(hit, gate, 0.0))
            rows.append(ref[window, :])
    total = lax.dot_general(
        jnp.concatenate(spread, axis=0).astype(bf16),
        jnp.concatenate(rows, axis=0),
        BY_ROWS,
        preferred_element_type=f32,
    )
    if rest:
        total = total + rest[0][0]
    out_ref[0] = total.astype(out_ref.dtype)


def merge_kernel(own_ref, got_ref, *outs):
    y = lax.axis_index("y")
    for s, out_ref in zip(STEPS, outs):
        there = lax.rem(y + s, NY)
        out_ref[...] = (own_ref[there] + got_ref[there].astype(f32)).astype(out_ref.dtype)


def final_kernel(hidden_ref, *refs):
    total = refs[0][...]
    for ref in refs[1:-1]:
        total = total + ref[...].astype(f32)
    refs[-1][...] = (hidden_ref[...].astype(f32) + total).astype(bf16)


def body(
    context,
    residual_in,
    out_weight,
    norm_gain,
    expert_ids,
    gate_weights,
    gate_matrix,
    lift_matrix,
    down_matrix,
):
    tokens, width = residual_in.shape
    top = expert_ids.shape[1]
    share = width // NX
    fine = share // NY
    units = gate_matrix.shape[2]
    capacity = min(tokens, max(2, tokens * top * 9 // (8 * NE)))
    blocks = NY * NC
    slots = blocks * capacity
    x = lax.axis_index("x")

    contexts = [shift(context, "y", NY, s) for s in STEPS]
    weight = jnp.concatenate(z_ring(out_weight.T), axis=0)
    packed = call(
        route_kernel,
        "route",
        [shape(tokens + TABLE, fine)] * NY,
        expert_ids.T,
        gate_weights.T,
        residual_in,
    )
    down_here, weight = lax.optimization_barrier((down_matrix[0], weight))
    downs = [
        lax.dynamic_slice_in_dim(down_here, lax.rem(x + s, NX) * share, share, 1) for s in STEPS
    ]
    weight, contexts = lax.optimization_barrier((weight, contexts))
    parts = call(
        project_kernel,
        "project",
        [shape(NY, tokens, fine, dtype=f32)] + [shape(NY, tokens, fine)] * (NX - 1),
        *contexts,
        weight,
        swap(weight),
        scratch=[pltpu.VMEM((NZ, NC * weight.shape[0] // NZ, share), bf16)],
        flops=2 * NY * tokens * share * width // NY,
    )
    parts, packed = lax.optimization_barrier((parts, packed))
    parts = x_exchange(parts)
    packed = y_exchange(packed)
    table = swap(call(pick_kernel, "pick", shape(NY, TABLE, tokens), *packed))
    parts, table, downs = lax.optimization_barrier((parts, table, downs))
    downs = x_exchange(downs)
    hidden = call(hidden_kernel, "hidden", shape(NY * tokens, fine), *parts, *packed)
    pieces = [shift(hidden, "y", NY, s) for s in STEPS]
    pieces, downs[1:3] = lax.optimization_barrier((pieces, downs[1:3]))
    hidden = call(gather_kernel, "gather", shape(NY * tokens, share), *pieces)
    *sent, own, table = call(
        functools.partial(dispatch_kernel, capacity),
        "dispatch",
        [shape(slots, share)] * NZ
        + [shape(tokens, share), shape(blocks, TABLE, tokens, dtype=f32)],
        *packed,
        table,
        hidden,
        swap(hidden),
        scratch=[pltpu.VMEM((blocks, TABLE, tokens), f32)],
        flops=2 * NZ * slots * blocks * tokens * share,
    )

    gain = norm_gain.astype(f32).reshape(NX, share)
    gate_here = gate_matrix.reshape(NX, share, units)
    lift_here = lift_matrix.reshape(NX, share, units)

    sent = dict(zip(SHIFTS, sent))
    got, rings, acts = [], [], []
    for i, group in enumerate(GROUPS):
        rows = [sent[s] for s in group]
        if i == 1:
            *rows, got[0] = lax.optimization_barrier((*rows, got[0]))
        elif i > 1:
            at, right, left, far = rings[i - 2]
            *rows, right, left = lax.optimization_barrier((*rows, right, left))
            rings[i - 2] = at, right, left, far
        rows = [shift(r, "z", NZ, s) for r, s in zip(rows, group)]
        if i > 1:
            at, right, left, far = rings[i - 2]
            *rows, far = lax.optimization_barrier((*rows, far))
            rings[i - 2] = at, right, left, far
        got.append(rows[0] if len(rows) == 1 else jnp.concatenate(rows, axis=0))
        if i > 0:
            rings.append(x_ring(got[i - 1], i - 1 in (0, 3)))
    rings.append(x_ring(got[-1], True))
    for i, ring in enumerate(rings):
        count = ring[0].shape[0]
        acts.append(
            call(
                functools.partial(up_kernel, width),
                f"up{i}",
                shape(count, units),
                *ring,
                gain,
                gate_here,
                lift_here,
                flops=4 * count * width * units,
            )
        )
    acts[0], downs[3] = lax.optimization_barrier((acts[0], downs[3]))
    total = None
    for i, group in enumerate(GROUPS):
        count = got[i].shape[0]
        back = call(
            down_kernel,
            f"down{i}",
            [shape(slots, share)] * len(group),
            *x_ring(acts[i], i in (0, 3)),
            *downs,
            flops=2 * count * NX * units * share,
            grid=(share // 256,),
            specs=(
                [pl.BlockSpec((count, units), lambda i: (0, 0))] * NX
                + [pl.BlockSpec((units, 256), lambda i: (0, i))] * NX,
                [pl.BlockSpec((slots, 256), lambda i: (0, i))] * len(group),
            ),
        )
        lists = [shift(r, "z", NZ, -s) for r, s in zip(back, group)]

        def combine(start, number, dtype, total=total, lists=lists, group=group, i=i):
            part = pl.BlockSpec((1, tokens, share), lambda b: (b, 0, 0))
            there = pl.BlockSpec((1, tokens, share), lambda b: (b + start, 0, 0))
            return call(
                functools.partial(combine_kernel, capacity, start, group),
                f"combine{i}_{start}",
                shape(number, tokens, share, dtype=dtype),
                table,
                *lists,
                *([] if total is None else [total]),
                flops=4 * len(group) * number * 32 * tokens * share,
                grid=(number,),
                specs=(
                    [pl.BlockSpec((1, TABLE, tokens), lambda b: (b + start, 0, 0))]
                    + [pl.BlockSpec((slots, share), lambda b: (0, 0))] * len(group)
                    + ([] if total is None else [there]),
                    part,
                ),
            )

        if i < len(GROUPS) - 1:
            total = combine(0, blocks, f32)
    crossing = combine(NY, NY, bf16)
    mine = combine(0, NY, f32)
    merged = call(
        merge_kernel,
        "merge",
        [shape(tokens, share, dtype=f32)] + [shape(tokens, share)] * (NY - 1),
        mine,
        swap(crossing),
    )
    return call(final_kernel, "final", shape(tokens, share), own, *y_exchange(merged))


def solution(mesh):
    fine = Mesh(mesh.devices.reshape(NZ, NY, NC, NX), ("z", "y", "c", "x"))
    e = ("z", "y", "c")
    placed = (
        P(e, "x"),
        P(e, None),
        P("x", e),
        P(),
        P(e, None),
        P(e, None),
        P(e, None, "x"),
        P(e, None, "x"),
        P(e, "x", None),
    )
    return jax.shard_map(body, mesh=fine, in_specs=placed, out_specs=P(e, "x"), check_vma=False)
```

```python
import functools

import jax
import jax.numpy as jnp
from jax import lax
from jax.experimental import pallas as pl
from jax.experimental.pallas import tpu as pltpu
from jax.sharding import Mesh
from jax.sharding import PartitionSpec as P

epsilon = 1e-06
f32 = jnp.float32
bf16 = jnp.bfloat16
NZ, NY, NC, NX = 8, 4, 2, 4
NE = NZ * NY * NC
STEPS = (0, 1, 3, 2)
GROUPS = ((0, 1, -1), (4,), (3, -3), (2, -2))
SHIFTS = sum(GROUPS, ())
RING = (0, 1, -1, 2, -2, 3, -3)
TABLE = 32
BY_ROWS = (((0,), (0,)), ((), ()))
BY_COLUMNS = (((1,), (1,)), ((), ()))


def shape(*dims, dtype=bf16):
    return jax.ShapeDtypeStruct(dims, dtype)


def call(kernel, name, outs, *args, scratch=(), mib=40, flops=0, grid=(), specs=None):
    size = sum(a.size * a.dtype.itemsize for a in args)
    blocks = {} if specs is None else dict(grid=grid, in_specs=specs[0], out_specs=specs[1])
    return pl.pallas_call(
        kernel,
        out_shape=outs,
        scratch_shapes=scratch,
        **blocks,
        compiler_params=pltpu.CompilerParams(vmem_limit_bytes=mib << 20),
        cost_estimate=pl.CostEstimate(flops=flops, bytes_accessed=size, transcendentals=0),
        name=name,
    )(*args)


def shift(value, axis, count, step):
    if step % count == 0:
        return value
    return lax.ppermute(value, axis, [(i, (i + step) % count) for i in range(count)])


def y_exchange(values):
    return [shift(v, "y", NY, s) for v, s in zip(values, STEPS)]


def x_exchange(values):
    return [shift(v, "x", NX, s) for v, s in zip(values, STEPS)]


def swap(value):
    return shift(value, "c", NC, 1)


def x_ring(value, way, *gate):
    right, left = shift(value, "x", NX, 1), shift(value, "x", NX, -1)
    right, left = lax.optimization_barrier((right, left))
    if gate:
        first, *_ = lax.optimization_barrier((right if way else left, *gate))
        right, left = (first, left) if way else (right, first)
    far = shift(right, "x", NX, 1) if way else shift(left, "x", NX, -1)
    return value, right, left, far


def z_ring(value):
    right = left = value
    pieces = [value]
    for _ in range(NZ // 2 - 1):
        right, left = shift(right, "z", NZ, 1), shift(left, "z", NZ, -1)
        pieces += [right, left]
    half = value.shape[0] // 2
    return pieces + [shift(right[:half], "z", NZ, 1), shift(left[half:], "z", NZ, -1)]


def route_kernel(ids_ref, gates_ref, residual_ref, *outs):
    tokens = ids_ref.shape[1]
    x, y = lax.axis_index("x"), lax.axis_index("y")
    row = lax.broadcasted_iota(jnp.int32, (NE, tokens), 0)
    group = row // (NC * NZ)
    step = group ^ (group >> 1)
    experts = (row % NZ) * (NY * NC) + ((y + step) % NY) * NC + (row // NZ) % NC
    chosen = jnp.zeros((NE, tokens), f32)
    weight = jnp.zeros((NE, tokens), f32)
    for k in range(ids_ref.shape[0]):
        same = experts == ids_ref[k : k + 1, :]
        chosen = jnp.where(same, 1.0, chosen)
        weight = jnp.where(same, gates_ref[k : k + 1, :], weight)
    rows = lax.broadcasted_iota(jnp.int32, (tokens, tokens), 0)
    columns = lax.broadcasted_iota(jnp.int32, (tokens, tokens), 1)
    before = jnp.where(rows < columns, 1.0, 0.0).astype(bf16)
    rank = jnp.dot(chosen.astype(bf16), before, preferred_element_type=f32)
    slot = jnp.where(chosen > 0.0, rank, -1.0)
    high = weight.astype(bf16).astype(f32)
    low = weight - high
    share = residual_ref.shape[1] // NX
    half, piece = share // 2, share // 8
    for i, (s, out_ref) in enumerate(zip(STEPS, outs)):
        there = lax.rem(y + s, NY)
        for b in range(2):
            column = pl.multiple_of(x * share + b * half + there * piece, piece)
            out_ref[:tokens, b * piece : (b + 1) * piece] = residual_ref[:, pl.ds(column, piece)]
        for c in range(NC):
            at = (i * NC + c) * NZ
            part = [t[at : at + NZ] for t in (slot, high, low)]
            part.append(jnp.zeros((NZ, tokens), f32))
            part = jnp.concatenate(part, axis=0).astype(bf16)
            out_ref[tokens:, c * tokens : (c + 1) * tokens] = part


def project_kernel(*refs):
    contexts, (mine_ref, other_ref), outs = refs[:NY], refs[NY : NY + 2], refs[NY + 2 : -1]
    all_ref = refs[-1]
    width = all_ref.shape[1] // NC
    x, z, c = lax.axis_index("x"), lax.axis_index("z"), lax.axis_index("c")
    for i in range(NZ):
        owner = lax.rem(z + NZ - (RING + (4,))[i], NZ)
        for ref, core in ((mine_ref, c), (other_ref, 1 - c)):
            there = pl.ds(pl.multiple_of(core * width, width), width)
            all_ref[owner, there, :] = ref[i * width : (i + 1) * width, :]
    for step, out_ref in zip(STEPS, outs):
        q = lax.rem(x + step, NX)
        weight = all_ref[pl.ds(2 * q, 2)].reshape(out_ref.shape[2], -1)
        for i, ref in enumerate(contexts):
            part = lax.dot_general(ref[...], weight, BY_COLUMNS, preferred_element_type=f32)
            out_ref[i] = part.astype(out_ref.dtype)


def hidden_kernel(*refs):
    parts, packed, out_ref = refs[:NX], refs[NX : NX + NY], refs[NX + NY]
    tokens = parts[0].shape[1]
    y = lax.axis_index("y")
    for i, s in enumerate(STEPS):
        total = parts[0][i]
        for ref in parts[1:]:
            total = total + ref[i].astype(f32)
        owner = lax.rem(y + NY - s, NY)
        residual = packed[i][:tokens, :].astype(f32)
        out_ref[pl.ds(pl.multiple_of(owner * tokens, tokens), tokens), :] = (
            residual + total
        ).astype(bf16)


def fill_table(packed, other_ref, table_ref):
    tokens = table_ref.shape[2]
    y, c = lax.axis_index("y"), lax.axis_index("c")
    mine = pl.ds(pl.multiple_of(c * tokens, tokens), tokens)
    for i, s in enumerate(STEPS):
        owner = lax.rem(y + NY - s, NY)
        table_ref[owner] = packed[i][-TABLE:, mine].astype(f32)
        table_ref[owner + NY] = other_ref[i].astype(f32)


def pick_kernel(*refs):
    packed, out_ref = refs[:NY], refs[NY]
    tokens = out_ref.shape[2]
    c = lax.axis_index("c")
    others = pl.ds(pl.multiple_of((1 - c) * tokens, tokens), tokens)
    for i in range(NY):
        out_ref[i] = packed[i][-TABLE:, others]


def gather_kernel(*refs):
    pieces, out_ref = refs[:NY], refs[NY]
    y = lax.axis_index("y")
    piece = pieces[0].shape[1] // 2
    half = out_ref.shape[1] // 2
    for ref, s in zip(pieces, STEPS):
        owner = lax.rem(y + NY - s, NY)
        for b in range(2):
            column = pl.multiple_of(b * half + owner * piece, piece)
            out_ref[:, pl.ds(column, piece)] = ref[:, b * piece : (b + 1) * piece]


def dispatch_kernel(capacity, *refs):
    packed, other_ref = refs[:NY], refs[NY]
    hidden_ref, across_ref = refs[NY + 1 : NY + 3]
    sent, (own_ref, table_out, table_ref) = refs[NY + 3 : -3], refs[-3:]
    tokens = own_ref.shape[0]
    blocks = NY * NC
    y, z = lax.axis_index("y"), lax.axis_index("z")
    fill_table(packed, other_ref, table_ref)
    table_out[...] = table_ref[...]
    own_ref[...] = hidden_ref[pl.ds(pl.multiple_of(y * tokens, tokens), tokens), :]
    slots = lax.broadcasted_iota(jnp.int32, (blocks * capacity, NY * tokens), 0)
    for s, out_ref in zip(SHIFTS, sent):
        d = lax.rem(z + NZ + s, NZ)
        rows = None
        for core, ref in enumerate((hidden_ref, across_ref)):
            parts = []
            for b in range(core * NY, core * NY + NY):
                slot = table_ref[b, pl.ds(d, 1), :]
                parts.append(jnp.where(slot >= 0.0, slot + float(b * capacity), -1.0))
            place = jnp.concatenate(parts, axis=1).astype(jnp.int32)
            pick = jnp.where(slots == place, 1.0, 0.0).astype(bf16)
            part = jnp.dot(pick, ref[...], preferred_element_type=f32)
            rows = part if rows is None else rows + part
        out_ref[...] = rows.astype(bf16)


def up_kernel(width, *refs):
    pieces, (gain_ref, gate_ref, lift_ref, out_ref) = refs[:NX], refs[NX:]
    x = lax.axis_index("x")
    squares = None
    for ref in pieces:
        h = ref[...].astype(f32)
        s = jnp.sum(h * h, axis=1, keepdims=True)
        squares = s if squares is None else squares + s
    scale = lax.rsqrt(squares * (1.0 / width) + epsilon)
    gate = lift = None
    for ref, back in zip(pieces, STEPS):
        q = lax.rem(x + NX - back, NX)
        normed = (ref[...].astype(f32) * scale * gain_ref[pl.ds(q, 1), :]).astype(bf16)
        g = jnp.dot(normed, gate_ref[q], preferred_element_type=f32)
        l = jnp.dot(normed, lift_ref[q], preferred_element_type=f32)
        gate = g if gate is None else gate + g
        lift = l if lift is None else lift + l
    out_ref[...] = (gate / (1.0 + jnp.exp(-gate)) * lift).astype(bf16)


def down_kernel(*refs):
    acts, downs, outs = refs[:NX], refs[NX : 2 * NX], refs[2 * NX :]
    total = None
    for act, down in zip(acts, downs):
        part = jnp.dot(act[...], down[...], preferred_element_type=f32)
        part = part.astype(bf16).astype(f32)
        total = part if total is None else total + part
    total = total.astype(bf16)
    rows = outs[0].shape[0]
    for i, out in enumerate(outs):
        out[...] = total[i * rows : (i + 1) * rows]


def combine_kernel(capacity, start, shifts, table_ref, *refs):
    lists, rest, out_ref = refs[: len(shifts)], refs[len(shifts) : -1], refs[-1]
    tokens = table_ref.shape[2]
    block = pl.program_id(0) + start
    z = lax.axis_index("z")
    first = (block * capacity) // 16 * 16
    window = pl.ds(pl.multiple_of(first, 16), 32)
    slots = lax.broadcasted_iota(jnp.int32, (32, tokens), 0) - (block * capacity - first)
    slots = slots.astype(f32)
    spread, rows = [], []
    for s, ref in zip(shifts, lists):
        d = lax.rem(z + NZ + s, NZ)
        hit = (slots == table_ref[0, pl.ds(d, 1), :]) & (slots >= 0.0)
        for part in (1, 2):
            gate = table_ref[0, pl.ds(part * NZ + d, 1), :]
            spread.append(jnp.where(hit, gate, 0.0))
            rows.append(ref[window, :])
    total = lax.dot_general(
        jnp.concatenate(spread, axis=0).astype(bf16),
        jnp.concatenate(rows, axis=0),
        BY_ROWS,
        preferred_element_type=f32,
    )
    if rest:
        total = total + rest[0][0]
    out_ref[0] = total.astype(out_ref.dtype)


def merge_kernel(own_ref, got_ref, *outs):
    y = lax.axis_index("y")
    for s, out_ref in zip(STEPS, outs):
        there = lax.rem(y + s, NY)
        out_ref[...] = (own_ref[there] + got_ref[there].astype(f32)).astype(out_ref.dtype)


def final_kernel(hidden_ref, *refs):
    total = refs[0][...]
    for ref in refs[1:-1]:
        total = total + ref[...].astype(f32)
    refs[-1][...] = (hidden_ref[...].astype(f32) + total).astype(bf16)


def body(
    context,
    residual_in,
    out_weight,
    norm_gain,
    expert_ids,
    gate_weights,
    gate_matrix,
    lift_matrix,
    down_matrix,
):
    tokens, width = residual_in.shape
    top = expert_ids.shape[1]
    share = width // NX
    fine = share // NY
    units = gate_matrix.shape[2]
    capacity = min(tokens, max(2, tokens * top * 9 // (8 * NE)))
    blocks = NY * NC
    slots = blocks * capacity
    x = lax.axis_index("x")

    contexts = [shift(context, "y", NY, s) for s in STEPS]
    weight = jnp.concatenate(z_ring(out_weight.T), axis=0)
    packed = call(
        route_kernel,
        "route",
        [shape(tokens + TABLE, fine)] * NY,
        expert_ids.T,
        gate_weights.T,
        residual_in,
    )
    down_here, weight = lax.optimization_barrier((down_matrix[0], weight))
    downs = [
        lax.dynamic_slice_in_dim(down_here, lax.rem(x + s, NX) * share, share, 1) for s in STEPS
    ]
    weight, contexts = lax.optimization_barrier((weight, contexts))
    parts = call(
        project_kernel,
        "project",
        [shape(NY, tokens, fine, dtype=f32)] + [shape(NY, tokens, fine)] * (NX - 1),
        *contexts,
        weight,
        swap(weight),
        scratch=[pltpu.VMEM((NZ, NC * weight.shape[0] // NZ, share), bf16)],
        flops=2 * NY * tokens * share * width // NY,
    )
    parts, packed = lax.optimization_barrier((parts, packed))
    parts = x_exchange(parts)
    packed = y_exchange(packed)
    table = swap(call(pick_kernel, "pick", shape(NY, TABLE, tokens), *packed))
    parts, table, downs = lax.optimization_barrier((parts, table, downs))
    downs = x_exchange(downs)
    hidden = call(hidden_kernel, "hidden", shape(NY * tokens, fine), *parts, *packed)
    pieces = [shift(hidden, "y", NY, s) for s in STEPS]
    pieces, downs[1:3] = lax.optimization_barrier((pieces, downs[1:3]))
    hidden = call(gather_kernel, "gather", shape(NY * tokens, share), *pieces)
    *sent, own, table = call(
        functools.partial(dispatch_kernel, capacity),
        "dispatch",
        [shape(slots, share)] * NZ
        + [shape(tokens, share), shape(blocks, TABLE, tokens, dtype=f32)],
        *packed,
        table,
        hidden,
        swap(hidden),
        scratch=[pltpu.VMEM((blocks, TABLE, tokens), f32)],
        flops=2 * NZ * slots * blocks * tokens * share,
    )

    gain = norm_gain.astype(f32).reshape(NX, share)
    gate_here = gate_matrix.reshape(NX, share, units)
    lift_here = lift_matrix.reshape(NX, share, units)

    sent = dict(zip(SHIFTS, sent))
    def up(i, ring):
        count = ring[0].shape[0]
        return call(
            functools.partial(up_kernel, width),
            f"up{i}",
            shape(count, units),
            *ring,
            gain,
            gate_here,
            lift_here,
            flops=4 * count * width * units,
        )

    got, rings, acts = [], [], []
    for i, group in enumerate(GROUPS):
        rows = [sent[s] for s in group]
        if i == 1:
            *rows, got[0] = lax.optimization_barrier((*rows, got[0]))
        elif i > 1:
            *rows, _, _ = lax.optimization_barrier((*rows, *rings[i - 2][1:3]))
        rows = [shift(r, "z", NZ, s) for r, s in zip(rows, group)]
        if i > 1:
            *rows, _ = lax.optimization_barrier((*rows, rings[i - 2][3]))
        got.append(rows[0] if len(rows) == 1 else jnp.concatenate(rows, axis=0))
        if i > 0:
            rings.append(x_ring(got[i - 1], i - 1 in (0, 3), *acts[: max(0, i - 2)]))
            acts.append(up(i - 1, rings[-1]))
    rings.append(x_ring(got[-1], True, *acts[:2]))
    acts.append(up(len(GROUPS) - 1, rings[-1]))
    acts[0], downs[3] = lax.optimization_barrier((acts[0], downs[3]))
    total = None
    for i, group in enumerate(GROUPS):
        count = got[i].shape[0]
        back = call(
            down_kernel,
            f"down{i}",
            [shape(slots, share)] * len(group),
            *x_ring(acts[i], i in (0, 3)),
            *downs,
            flops=2 * count * NX * units * share,
            grid=(share // 256,),
            specs=(
                [pl.BlockSpec((count, units), lambda i: (0, 0))] * NX
                + [pl.BlockSpec((units, 256), lambda i: (0, i))] * NX,
                [pl.BlockSpec((slots, 256), lambda i: (0, i))] * len(group),
            ),
        )
        lists = [shift(r, "z", NZ, -s) for r, s in zip(back, group)]

        def combine(start, number, dtype, total=total, lists=lists, group=group, i=i):
            part = pl.BlockSpec((1, tokens, share), lambda b: (b, 0, 0))
            there = pl.BlockSpec((1, tokens, share), lambda b: (b + start, 0, 0))
            return call(
                functools.partial(combine_kernel, capacity, start, group),
                f"combine{i}_{start}",
                shape(number, tokens, share, dtype=dtype),
                table,
                *lists,
                *([] if total is None else [total]),
                flops=4 * len(group) * number * 32 * tokens * share,
                grid=(number,),
                specs=(
                    [pl.BlockSpec((1, TABLE, tokens), lambda b: (b + start, 0, 0))]
                    + [pl.BlockSpec((slots, share), lambda b: (0, 0))] * len(group)
                    + ([] if total is None else [there]),
                    part,
                ),
            )

        if i < len(GROUPS) - 1:
            total = combine(0, blocks, f32)
    crossing = combine(NY, NY, bf16)
    mine = combine(0, NY, f32)
    merged = call(
        merge_kernel,
        "merge",
        [shape(tokens, share, dtype=f32)] + [shape(tokens, share)] * (NY - 1),
        mine,
        swap(crossing),
    )
    return call(final_kernel, "final", shape(tokens, share), own, *y_exchange(merged))


def solution(mesh):
    fine = Mesh(mesh.devices.reshape(NZ, NY, NC, NX), ("z", "y", "c", "x"))
    e = ("z", "y", "c")
    placed = (
        P(e, "x"),
        P(e, None),
        P("x", e),
        P(),
        P(e, None),
        P(e, None),
        P(e, None, "x"),
        P(e, None, "x"),
        P(e, "x", None),
    )
    return jax.shard_map(body, mesh=fine, in_specs=placed, out_specs=P(e, "x"), check_vma=False)
```

```python
import functools

import jax
import jax.numpy as jnp
from jax import lax
from jax.experimental import pallas as pl
from jax.experimental.pallas import tpu as pltpu
from jax.sharding import Mesh
from jax.sharding import PartitionSpec as P

epsilon = 1e-06
f32 = jnp.float32
bf16 = jnp.bfloat16
NZ, NY, NC, NX = 8, 4, 2, 4
NE = NZ * NY * NC
STEPS = (0, 1, 3, 2)
GROUPS = ((0, 1, -1), (4,), (3, -3), (2, -2))
SHIFTS = sum(GROUPS, ())
RING = (0, 1, -1, 2, -2, 3, -3)
TABLE = 32
BY_ROWS = (((0,), (0,)), ((), ()))
BY_COLUMNS = (((1,), (1,)), ((), ()))


def shape(*dims, dtype=bf16):
    return jax.ShapeDtypeStruct(dims, dtype)


def call(kernel, name, outs, *args, scratch=(), mib=24, flops=0, grid=(), specs=None):
    size = sum(a.size * a.dtype.itemsize for a in args)
    blocks = {} if specs is None else dict(grid=grid, in_specs=specs[0], out_specs=specs[1])
    return pl.pallas_call(
        kernel,
        out_shape=outs,
        scratch_shapes=scratch,
        **blocks,
        compiler_params=pltpu.CompilerParams(vmem_limit_bytes=mib << 20),
        cost_estimate=pl.CostEstimate(flops=flops, bytes_accessed=size, transcendentals=0),
        name=name,
    )(*args)


def shift(value, axis, count, step):
    if step % count == 0:
        return value
    return lax.ppermute(value, axis, [(i, (i + step) % count) for i in range(count)])


def y_exchange(values):
    return [shift(v, "y", NY, s) for v, s in zip(values, STEPS)]


def x_exchange(values):
    return [shift(v, "x", NX, s) for v, s in zip(values, STEPS)]


def swap(value):
    return shift(value, "c", NC, 1)


def x_ring(value, way):
    right, left = shift(value, "x", NX, 1), shift(value, "x", NX, -1)
    right, left = lax.optimization_barrier((right, left))
    far = shift(right, "x", NX, 1) if way else shift(left, "x", NX, -1)
    return value, right, left, far


def z_ring(value):
    right = left = value
    pieces = [value]
    for _ in range(NZ // 2 - 1):
        right, left = shift(right, "z", NZ, 1), shift(left, "z", NZ, -1)
        pieces += [right, left]
    half = value.shape[0] // 2
    return pieces + [shift(right[:half], "z", NZ, 1), shift(left[half:], "z", NZ, -1)]


def route_kernel(ids_ref, gates_ref, residual_ref, *outs):
    tokens = ids_ref.shape[1]
    x, y = lax.axis_index("x"), lax.axis_index("y")
    row = lax.broadcasted_iota(jnp.int32, (NE, tokens), 0)
    group = row // (NC * NZ)
    step = group ^ (group >> 1)
    experts = (row % NZ) * (NY * NC) + ((y + step) % NY) * NC + (row // NZ) % NC
    chosen = jnp.zeros((NE, tokens), f32)
    weight = jnp.zeros((NE, tokens), f32)
    for k in range(ids_ref.shape[0]):
        same = experts == ids_ref[k : k + 1, :]
        chosen = jnp.where(same, 1.0, chosen)
        weight = jnp.where(same, gates_ref[k : k + 1, :], weight)
    rows = lax.broadcasted_iota(jnp.int32, (tokens, tokens), 0)
    columns = lax.broadcasted_iota(jnp.int32, (tokens, tokens), 1)
    before = jnp.where(rows < columns, 1.0, 0.0).astype(bf16)
    rank = jnp.dot(chosen.astype(bf16), before, preferred_element_type=f32)
    slot = jnp.where(chosen > 0.0, rank, -1.0)
    high = weight.astype(bf16).astype(f32)
    low = weight - high
    share = residual_ref.shape[1] // NX
    half, piece = share // 2, share // 8
    for i, (s, out_ref) in enumerate(zip(STEPS, outs)):
        there = lax.rem(y + s, NY)
        for b in range(2):
            column = pl.multiple_of(x * share + b * half + there * piece, piece)
            out_ref[:tokens, b * piece : (b + 1) * piece] = residual_ref[:, pl.ds(column, piece)]
        for c in range(NC):
            at = (i * NC + c) * NZ
            part = [t[at : at + NZ] for t in (slot, high, low)]
            part.append(jnp.zeros((NZ, tokens), f32))
            part = jnp.concatenate(part, axis=0).astype(bf16)
            out_ref[tokens:, c * tokens : (c + 1) * tokens] = part


def project_kernel(*refs):
    contexts, (mine_ref, other_ref), outs = refs[:NY], refs[NY : NY + 2], refs[NY + 2 : -1]
    all_ref = refs[-1]
    width = all_ref.shape[1] // NC
    x, z, c = lax.axis_index("x"), lax.axis_index("z"), lax.axis_index("c")
    for i in range(NZ):
        owner = lax.rem(z + NZ - (RING + (4,))[i], NZ)
        for ref, core in ((mine_ref, c), (other_ref, 1 - c)):
            there = pl.ds(pl.multiple_of(core * width, width), width)
            all_ref[owner, there, :] = ref[i * width : (i + 1) * width, :]
    for step, out_ref in zip(STEPS, outs):
        q = lax.rem(x + step, NX)
        weight = all_ref[pl.ds(2 * q, 2)].reshape(out_ref.shape[2], -1)
        for i, ref in enumerate(contexts):
            part = lax.dot_general(ref[...], weight, BY_COLUMNS, preferred_element_type=f32)
            out_ref[i] = part.astype(out_ref.dtype)


def hidden_kernel(*refs):
    parts, packed, out_ref = refs[:NX], refs[NX : NX + NY], refs[NX + NY]
    tokens = parts[0].shape[1]
    y = lax.axis_index("y")
    for i, s in enumerate(STEPS):
        total = parts[0][i]
        for ref in parts[1:]:
            total = total + ref[i].astype(f32)
        owner = lax.rem(y + NY - s, NY)
        residual = packed[i][:tokens, :].astype(f32)
        out_ref[pl.ds(pl.multiple_of(owner * tokens, tokens), tokens), :] = (
            residual + total
        ).astype(bf16)


def fill_table(packed, other_ref, table_ref):
    tokens = table_ref.shape[2]
    y, c = lax.axis_index("y"), lax.axis_index("c")
    mine = pl.ds(pl.multiple_of(c * tokens, tokens), tokens)
    for i, s in enumerate(STEPS):
        owner = lax.rem(y + NY - s, NY)
        table_ref[owner] = packed[i][-TABLE:, mine].astype(f32)
        table_ref[owner + NY] = other_ref[i].astype(f32)


def pick_kernel(*refs):
    packed, out_ref = refs[:NY], refs[NY]
    tokens = out_ref.shape[2]
    c = lax.axis_index("c")
    others = pl.ds(pl.multiple_of((1 - c) * tokens, tokens), tokens)
    for i in range(NY):
        out_ref[i] = packed[i][-TABLE:, others]


def gather_kernel(*refs):
    pieces, out_ref = refs[:NY], refs[NY]
    y = lax.axis_index("y")
    piece = pieces[0].shape[1] // 2
    half = out_ref.shape[1] // 2
    for ref, s in zip(pieces, STEPS):
        owner = lax.rem(y + NY - s, NY)
        for b in range(2):
            column = pl.multiple_of(b * half + owner * piece, piece)
            out_ref[:, pl.ds(column, piece)] = ref[:, b * piece : (b + 1) * piece]


def dispatch_kernel(capacity, *refs):
    packed, other_ref = refs[:NY], refs[NY]
    hidden_ref, across_ref = refs[NY + 1 : NY + 3]
    sent, (own_ref, table_out, table_ref) = refs[NY + 3 : -3], refs[-3:]
    tokens = own_ref.shape[0]
    blocks = NY * NC
    y, z = lax.axis_index("y"), lax.axis_index("z")
    fill_table(packed, other_ref, table_ref)
    table_out[...] = table_ref[...]
    own_ref[...] = hidden_ref[pl.ds(pl.multiple_of(y * tokens, tokens), tokens), :]
    slots = lax.broadcasted_iota(jnp.int32, (blocks * capacity, NY * tokens), 0)
    for s, out_ref in zip(SHIFTS, sent):
        d = lax.rem(z + NZ + s, NZ)
        rows = None
        for core, ref in enumerate((hidden_ref, across_ref)):
            parts = []
            for b in range(core * NY, core * NY + NY):
                slot = table_ref[b, pl.ds(d, 1), :]
                parts.append(jnp.where(slot >= 0.0, slot + float(b * capacity), -1.0))
            place = jnp.concatenate(parts, axis=1).astype(jnp.int32)
            pick = jnp.where(slots == place, 1.0, 0.0).astype(bf16)
            part = jnp.dot(pick, ref[...], preferred_element_type=f32)
            rows = part if rows is None else rows + part
        out_ref[...] = rows.astype(bf16)


def join_kernel(*refs):
    row = 0
    for ref in refs[:-1]:
        refs[-1][row : row + ref.shape[0], :] = ref[...]
        row += ref.shape[0]


def cut_kernel(down_ref, *outs):
    share = outs[0].shape[1]
    x = lax.axis_index("x")
    for s, out_ref in zip(STEPS, outs):
        first = pl.multiple_of(lax.rem(x + s, NX) * share, share)
        out_ref[...] = down_ref[:, pl.ds(first, share)]


def up_kernel(width, *refs):
    pieces, (gain_ref, gate_ref, lift_ref, out_ref) = refs[:NX], refs[NX:]
    x = lax.axis_index("x")
    squares = None
    for ref in pieces:
        h = ref[...].astype(f32)
        s = jnp.sum(h * h, axis=1, keepdims=True)
        squares = s if squares is None else squares + s
    scale = lax.rsqrt(squares * (1.0 / width) + epsilon)
    gate = lift = None
    for ref, back in zip(pieces, STEPS):
        q = lax.rem(x + NX - back, NX)
        normed = (ref[...].astype(f32) * scale * gain_ref[pl.ds(q, 1), :]).astype(bf16)
        g = jnp.dot(normed, gate_ref[q], preferred_element_type=f32)
        l = jnp.dot(normed, lift_ref[q], preferred_element_type=f32)
        gate = g if gate is None else gate + g
        lift = l if lift is None else lift + l
    out_ref[...] = (gate / (1.0 + jnp.exp(-gate)) * lift).astype(bf16)


def down_kernel(*refs):
    acts, downs, outs = refs[:NX], refs[NX : 2 * NX], refs[2 * NX :]
    total = None
    for act, down in zip(acts, downs):
        part = jnp.dot(act[...], down[...], preferred_element_type=f32)
        part = part.astype(bf16).astype(f32)
        total = part if total is None else total + part
    total = total.astype(bf16)
    rows = outs[0].shape[0]
    for i, out in enumerate(outs):
        out[...] = total[i * rows : (i + 1) * rows]


def combine_kernel(capacity, start, shifts, table_ref, *refs):
    lists, rest, out_ref = refs[: len(shifts)], refs[len(shifts) : -1], refs[-1]
    tokens = table_ref.shape[2]
    block = pl.program_id(0) + start
    z = lax.axis_index("z")
    first = (block * capacity) // 16 * 16
    window = pl.ds(pl.multiple_of(first, 16), 32)
    slots = lax.broadcasted_iota(jnp.int32, (32, tokens), 0) - (block * capacity - first)
    slots = slots.astype(f32)
    spread, rows = [], []
    for s, ref in zip(shifts, lists):
        d = lax.rem(z + NZ + s, NZ)
        hit = (slots == table_ref[0, pl.ds(d, 1), :]) & (slots >= 0.0)
        for part in (1, 2):
            gate = table_ref[0, pl.ds(part * NZ + d, 1), :]
            spread.append(jnp.where(hit, gate, 0.0))
            rows.append(ref[window, :])
    total = lax.dot_general(
        jnp.concatenate(spread, axis=0).astype(bf16),
        jnp.concatenate(rows, axis=0),
        BY_ROWS,
        preferred_element_type=f32,
    )
    if rest:
        total = total + rest[0][0]
    out_ref[0] = total.astype(out_ref.dtype)


def merge_kernel(own_ref, got_ref, *outs):
    y = lax.axis_index("y")
    for s, out_ref in zip(STEPS, outs):
        there = lax.rem(y + s, NY)
        out_ref[...] = (own_ref[there] + got_ref[there].astype(f32)).astype(out_ref.dtype)


def final_kernel(hidden_ref, *refs):
    total = refs[0][...]
    for ref in refs[1:-1]:
        total = total + ref[...].astype(f32)
    refs[-1][...] = (hidden_ref[...].astype(f32) + total).astype(bf16)


def body(
    context,
    residual_in,
    out_weight,
    norm_gain,
    expert_ids,
    gate_weights,
    gate_matrix,
    lift_matrix,
    down_matrix,
):
    tokens, width = residual_in.shape
    top = expert_ids.shape[1]
    share = width // NX
    fine = share // NY
    units = gate_matrix.shape[2]
    capacity = min(tokens, max(2, tokens * top * 9 // (8 * NE)))
    blocks = NY * NC
    slots = blocks * capacity
    contexts = [shift(context, "y", NY, s) for s in STEPS]
    weight = jnp.concatenate(z_ring(out_weight.T), axis=0)
    packed = call(
        route_kernel,
        "route",
        [shape(tokens + TABLE, fine)] * NY,
        expert_ids.T,
        gate_weights.T,
        residual_in,
    )
    down_here, weight = lax.optimization_barrier((down_matrix[0], weight))
    downs = call(cut_kernel, "cut", [shape(units, share)] * NX, down_here)
    gain = norm_gain.astype(f32).reshape(NX, share)
    gain, contexts[0] = lax.optimization_barrier((gain, contexts[0]))
    weight, contexts = lax.optimization_barrier((weight, contexts))
    parts = call(
        project_kernel,
        "project",
        [shape(NY, tokens, fine, dtype=f32)] + [shape(NY, tokens, fine)] * (NX - 1),
        *contexts,
        weight,
        swap(weight),
        scratch=[pltpu.VMEM((NZ, NC * weight.shape[0] // NZ, share), bf16)],
        flops=2 * NY * tokens * share * width // NY,
    )
    parts, packed = lax.optimization_barrier((parts, packed))
    parts = x_exchange(parts)
    packed = y_exchange(packed)
    table = swap(call(pick_kernel, "pick", shape(NY, TABLE, tokens), *packed))
    parts, table, downs = lax.optimization_barrier((parts, table, downs))
    downs = x_exchange(downs)
    hidden = call(hidden_kernel, "hidden", shape(NY * tokens, fine), *parts, *packed)
    pieces = [shift(hidden, "y", NY, s) for s in STEPS]
    pieces, downs[1:3] = lax.optimization_barrier((pieces, downs[1:3]))
    hidden = call(gather_kernel, "gather", shape(NY * tokens, share), *pieces)
    *sent, own, table = call(
        functools.partial(dispatch_kernel, capacity),
        "dispatch",
        [shape(slots, share)] * NZ
        + [shape(tokens, share), shape(blocks, TABLE, tokens, dtype=f32)],
        *packed,
        table,
        hidden,
        swap(hidden),
        scratch=[pltpu.VMEM((blocks, TABLE, tokens), f32)],
        flops=2 * NZ * slots * blocks * tokens * share,
    )

    gate_here = gate_matrix.reshape(NX, share, units)
    lift_here = lift_matrix.reshape(NX, share, units)

    sent = dict(zip(SHIFTS, sent))
    got, rings, acts = [], [], []
    for i, group in enumerate(GROUPS):
        rows = [sent[s] for s in group]
        if i == 1:
            *rows, got[0] = lax.optimization_barrier((*rows, got[0]))
        elif i > 1:
            at, right, left, far = rings[i - 2]
            *rows, right, left = lax.optimization_barrier((*rows, right, left))
            rings[i - 2] = at, right, left, far
        rows = [shift(r, "z", NZ, s) for r, s in zip(rows, group)]
        if i > 1:
            at, right, left, far = rings[i - 2]
            *rows, far = lax.optimization_barrier((*rows, far))
            rings[i - 2] = at, right, left, far
        count = len(group) * slots
        got.append(rows[0] if len(rows) == 1 else call(join_kernel, f"join{i}", shape(count, share), *rows, mib=8))
        if i > 0:
            rings.append(x_ring(got[i - 1], i - 1 in (0, 3)))
    rings.append(x_ring(got[-1], True))
    for i, ring in enumerate(rings):
        count = ring[0].shape[0]
        acts.append(
            call(
                functools.partial(up_kernel, width),
                f"up{i}",
                shape(count, units),
                *ring,
                gain,
                gate_here,
                lift_here,
                flops=4 * count * width * units,
            )
        )
    acts[0], downs[3] = lax.optimization_barrier((acts[0], downs[3]))
    total = None
    for i, group in enumerate(GROUPS):
        count = got[i].shape[0]
        back = call(
            down_kernel,
            f"down{i}",
            [shape(slots, share)] * len(group),
            *x_ring(acts[i], i in (0, 3)),
            *downs,
            flops=2 * count * NX * units * share,
            grid=(share // 256,),
            specs=(
                [pl.BlockSpec((count, units), lambda i: (0, 0))] * NX
                + [pl.BlockSpec((units, 256), lambda i: (0, i))] * NX,
                [pl.BlockSpec((slots, 256), lambda i: (0, i))] * len(group),
            ),
        )
        lists = [shift(r, "z", NZ, -s) for r, s in zip(back, group)]

        def combine(start, number, dtype, total=total, lists=lists, group=group, i=i):
            part = pl.BlockSpec((1, tokens, share), lambda b: (b, 0, 0))
            there = pl.BlockSpec((1, tokens, share), lambda b: (b + start, 0, 0))
            return call(
                functools.partial(combine_kernel, capacity, start, group),
                f"combine{i}_{start}",
                shape(number, tokens, share, dtype=dtype),
                table,
                *lists,
                *([] if total is None else [total]),
                flops=4 * len(group) * number * 32 * tokens * share,
                grid=(number,),
                specs=(
                    [pl.BlockSpec((1, TABLE, tokens), lambda b: (b + start, 0, 0))]
                    + [pl.BlockSpec((slots, share), lambda b: (0, 0))] * len(group)
                    + ([] if total is None else [there]),
                    part,
                ),
            )

        if i < len(GROUPS) - 1:
            total = combine(0, blocks, f32)
    crossing = combine(NY, NY, bf16)
    mine = combine(0, NY, f32)
    merged = call(
        merge_kernel,
        "merge",
        [shape(tokens, share, dtype=f32)] + [shape(tokens, share)] * (NY - 1),
        mine,
        swap(crossing),
    )
    return call(final_kernel, "final", shape(tokens, share), own, *y_exchange(merged))


def solution(mesh):
    fine = Mesh(mesh.devices.reshape(NZ, NY, NC, NX), ("z", "y", "c", "x"))
    e = ("z", "y", "c")
    placed = (
        P(e, "x"),
        P(e, None),
        P("x", e),
        P(),
        P(e, None),
        P(e, None),
        P(e, None, "x"),
        P(e, None, "x"),
        P(e, "x", None),
    )
    return jax.shard_map(body, mesh=fine, in_specs=placed, out_specs=P(e, "x"), check_vma=False)
```

```python
import functools

import jax
import jax.numpy as jnp
from jax import lax
from jax.experimental import pallas as pl
from jax.experimental.pallas import tpu as pltpu
from jax.sharding import Mesh
from jax.sharding import PartitionSpec as P

epsilon = 1e-06
f32 = jnp.float32
bf16 = jnp.bfloat16
NZ, NY, NC, NX = 8, 4, 2, 4
NE = NZ * NY * NC
STEPS = (0, 1, 3, 2)
GROUPS = ((0, 1, -1), (4,), (3, -3), (2, -2))
SHIFTS = sum(GROUPS, ())
RING = (0, 1, -1, 2, -2, 3, -3)
TABLE = 32
BY_ROWS = (((0,), (0,)), ((), ()))
BY_COLUMNS = (((1,), (1,)), ((), ()))


def shape(*dims, dtype=bf16):
    return jax.ShapeDtypeStruct(dims, dtype)


def call(kernel, name, outs, *args, scratch=(), mib=24, flops=0, grid=(), specs=None):
    size = sum(a.size * a.dtype.itemsize for a in args)
    blocks = {} if specs is None else dict(grid=grid, in_specs=specs[0], out_specs=specs[1])
    return pl.pallas_call(
        kernel,
        out_shape=outs,
        scratch_shapes=scratch,
        **blocks,
        compiler_params=pltpu.CompilerParams(vmem_limit_bytes=mib << 20),
        cost_estimate=pl.CostEstimate(flops=flops, bytes_accessed=size, transcendentals=0),
        name=name,
    )(*args)


def shift(value, axis, count, step):
    if step % count == 0:
        return value
    return lax.ppermute(value, axis, [(i, (i + step) % count) for i in range(count)])


def y_exchange(values):
    return [shift(v, "y", NY, s) for v, s in zip(values, STEPS)]


def x_exchange(values):
    return [shift(v, "x", NX, s) for v, s in zip(values, STEPS)]


def swap(value):
    return shift(value, "c", NC, 1)


def x_ring(value, way):
    right, left = shift(value, "x", NX, 1), shift(value, "x", NX, -1)
    right, left = lax.optimization_barrier((right, left))
    far = shift(right, "x", NX, 1) if way else shift(left, "x", NX, -1)
    return value, right, left, far


def z_ring(value):
    right = left = value
    pieces = [value]
    for _ in range(NZ // 2 - 1):
        right, left = shift(right, "z", NZ, 1), shift(left, "z", NZ, -1)
        pieces += [right, left]
    half = value.shape[0] // 2
    return pieces + [shift(right[:half], "z", NZ, 1), shift(left[half:], "z", NZ, -1)]


def route_kernel(ids_ref, gates_ref, residual_ref, *outs):
    tokens = ids_ref.shape[1]
    x, y = lax.axis_index("x"), lax.axis_index("y")
    row = lax.broadcasted_iota(jnp.int32, (NE, tokens), 0)
    group = row // (NC * NZ)
    step = group ^ (group >> 1)
    experts = (row % NZ) * (NY * NC) + ((y + step) % NY) * NC + (row // NZ) % NC
    chosen = jnp.zeros((NE, tokens), f32)
    weight = jnp.zeros((NE, tokens), f32)
    for k in range(ids_ref.shape[0]):
        same = experts == ids_ref[k : k + 1, :]
        chosen = jnp.where(same, 1.0, chosen)
        weight = jnp.where(same, gates_ref[k : k + 1, :], weight)
    rows = lax.broadcasted_iota(jnp.int32, (tokens, tokens), 0)
    columns = lax.broadcasted_iota(jnp.int32, (tokens, tokens), 1)
    before = jnp.where(rows < columns, 1.0, 0.0).astype(bf16)
    rank = jnp.dot(chosen.astype(bf16), before, preferred_element_type=f32)
    slot = jnp.where(chosen > 0.0, rank, -1.0)
    high = weight.astype(bf16).astype(f32)
    low = weight - high
    share = residual_ref.shape[1] // NX
    half, piece = share // 2, share // 8
    for i, (s, out_ref) in enumerate(zip(STEPS, outs)):
        there = lax.rem(y + s, NY)
        for b in range(2):
            column = pl.multiple_of(x * share + b * half + there * piece, piece)
            out_ref[:tokens, b * piece : (b + 1) * piece] = residual_ref[:, pl.ds(column, piece)]
        for c in range(NC):
            at = (i * NC + c) * NZ
            part = [t[at : at + NZ] for t in (slot, high, low)]
            part.append(jnp.zeros((NZ, tokens), f32))
            part = jnp.concatenate(part, axis=0).astype(bf16)
            out_ref[tokens:, c * tokens : (c + 1) * tokens] = part


def project_kernel(*refs):
    contexts, (mine_ref, other_ref), outs = refs[:NY], refs[NY : NY + 2], refs[NY + 2 : -1]
    all_ref = refs[-1]
    width = all_ref.shape[1] // NC
    x, z, c = lax.axis_index("x"), lax.axis_index("z"), lax.axis_index("c")
    for i in range(NZ):
        owner = lax.rem(z + NZ - (RING + (4,))[i], NZ)
        for ref, core in ((mine_ref, c), (other_ref, 1 - c)):
            there = pl.ds(pl.multiple_of(core * width, width), width)
            all_ref[owner, there, :] = ref[i * width : (i + 1) * width, :]
    for step, out_ref in zip(STEPS, outs):
        q = lax.rem(x + step, NX)
        weight = all_ref[pl.ds(2 * q, 2)].reshape(out_ref.shape[2], -1)
        for i, ref in enumerate(contexts):
            part = lax.dot_general(ref[...], weight, BY_COLUMNS, preferred_element_type=f32)
            out_ref[i] = part.astype(out_ref.dtype)


def hidden_kernel(*refs):
    parts, packed, out_ref = refs[:NX], refs[NX : NX + NY], refs[NX + NY]
    tokens = parts[0].shape[1]
    y = lax.axis_index("y")
    for i, s in enumerate(STEPS):
        total = parts[0][i]
        for ref in parts[1:]:
            total = total + ref[i].astype(f32)
        owner = lax.rem(y + NY - s, NY)
        residual = packed[i][:tokens, :].astype(f32)
        out_ref[pl.ds(pl.multiple_of(owner * tokens, tokens), tokens), :] = (
            residual + total
        ).astype(bf16)


def fill_table(packed, other_ref, table_ref):
    tokens = table_ref.shape[2]
    y, c = lax.axis_index("y"), lax.axis_index("c")
    mine = pl.ds(pl.multiple_of(c * tokens, tokens), tokens)
    for i, s in enumerate(STEPS):
        owner = lax.rem(y + NY - s, NY)
        table_ref[owner] = packed[i][-TABLE:, mine].astype(f32)
        table_ref[owner + NY] = other_ref[i].astype(f32)


def pick_kernel(*refs):
    packed, out_ref = refs[:NY], refs[NY]
    tokens = out_ref.shape[2]
    c = lax.axis_index("c")
    others = pl.ds(pl.multiple_of((1 - c) * tokens, tokens), tokens)
    for i in range(NY):
        out_ref[i] = packed[i][-TABLE:, others]


def gather_kernel(*refs):
    pieces, out_ref = refs[:NY], refs[NY]
    y = lax.axis_index("y")
    piece = pieces[0].shape[1] // 2
    half = out_ref.shape[1] // 2
    for ref, s in zip(pieces, STEPS):
        owner = lax.rem(y + NY - s, NY)
        for b in range(2):
            column = pl.multiple_of(b * half + owner * piece, piece)
            out_ref[:, pl.ds(column, piece)] = ref[:, b * piece : (b + 1) * piece]


def dispatch_kernel(capacity, *refs):
    packed, other_ref = refs[:NY], refs[NY]
    hidden_ref, across_ref = refs[NY + 1 : NY + 3]
    sent, (own_ref, table_out, table_ref) = refs[NY + 3 : -3], refs[-3:]
    tokens = own_ref.shape[0]
    blocks = NY * NC
    y, z = lax.axis_index("y"), lax.axis_index("z")
    fill_table(packed, other_ref, table_ref)
    table_out[...] = table_ref[...]
    own_ref[...] = hidden_ref[pl.ds(pl.multiple_of(y * tokens, tokens), tokens), :]
    slots = lax.broadcasted_iota(jnp.int32, (blocks * capacity, NY * tokens), 0)
    for s, out_ref in zip(SHIFTS, sent):
        d = lax.rem(z + NZ + s, NZ)
        rows = None
        for core, ref in enumerate((hidden_ref, across_ref)):
            parts = []
            for b in range(core * NY, core * NY + NY):
                slot = table_ref[b, pl.ds(d, 1), :]
                parts.append(jnp.where(slot >= 0.0, slot + float(b * capacity), -1.0))
            place = jnp.concatenate(parts, axis=1).astype(jnp.int32)
            pick = jnp.where(slots == place, 1.0, 0.0).astype(bf16)
            part = jnp.dot(pick, ref[...], preferred_element_type=f32)
            rows = part if rows is None else rows + part
        out_ref[...] = rows.astype(bf16)


def join_kernel(*refs):
    row = 0
    for ref in refs[:-1]:
        refs[-1][row : row + ref.shape[0], :] = ref[...]
        row += ref.shape[0]


def cut_kernel(down_ref, *outs):
    share = outs[0].shape[1]
    x = lax.axis_index("x")
    for s, out_ref in zip(STEPS, outs):
        first = pl.multiple_of(lax.rem(x + s, NX) * share, share)
        out_ref[...] = down_ref[:, pl.ds(first, share)]


def up_kernel(width, *refs):
    pieces, (gain_ref, gate_ref, lift_ref, out_ref) = refs[:NX], refs[NX:]
    x = lax.axis_index("x")
    squares = None
    for ref in pieces:
        h = ref[...].astype(f32)
        s = jnp.sum(h * h, axis=1, keepdims=True)
        squares = s if squares is None else squares + s
    scale = lax.rsqrt(squares * (1.0 / width) + epsilon)
    gate = lift = None
    for ref, back in zip(pieces, STEPS):
        q = lax.rem(x + NX - back, NX)
        normed = (ref[...].astype(f32) * scale * gain_ref[pl.ds(q, 1), :]).astype(bf16)
        g = jnp.dot(normed, gate_ref[q], preferred_element_type=f32)
        l = jnp.dot(normed, lift_ref[q], preferred_element_type=f32)
        gate = g if gate is None else gate + g
        lift = l if lift is None else lift + l
    out_ref[...] = (gate / (1.0 + jnp.exp(-gate)) * lift).astype(bf16)


def down_kernel(*refs):
    acts, downs, outs = refs[:NX], refs[NX : 2 * NX], refs[2 * NX :]
    total = None
    for act, down in zip(acts, downs):
        part = jnp.dot(act[...], down[...], preferred_element_type=f32)
        part = part.astype(bf16).astype(f32)
        total = part if total is None else total + part
    total = total.astype(bf16)
    rows = outs[0].shape[0]
    for i, out in enumerate(outs):
        out[...] = total[i * rows : (i + 1) * rows]


def combine_kernel(capacity, start, shifts, table_ref, *refs):
    lists, rest, out_ref = refs[: len(shifts)], refs[len(shifts) : -1], refs[-1]
    tokens = table_ref.shape[2]
    block = pl.program_id(0) + start
    z = lax.axis_index("z")
    first = (block * capacity) // 16 * 16
    window = pl.ds(pl.multiple_of(first, 16), 32)
    slots = lax.broadcasted_iota(jnp.int32, (32, tokens), 0) - (block * capacity - first)
    slots = slots.astype(f32)
    spread, rows = [], []
    for s, ref in zip(shifts, lists):
        d = lax.rem(z + NZ + s, NZ)
        hit = (slots == table_ref[0, pl.ds(d, 1), :]) & (slots >= 0.0)
        for part in (1, 2):
            gate = table_ref[0, pl.ds(part * NZ + d, 1), :]
            spread.append(jnp.where(hit, gate, 0.0))
            rows.append(ref[window, :])
    total = lax.dot_general(
        jnp.concatenate(spread, axis=0).astype(bf16),
        jnp.concatenate(rows, axis=0),
        BY_ROWS,
        preferred_element_type=f32,
    )
    if rest:
        total = total + rest[0][0]
    out_ref[0] = total.astype(out_ref.dtype)


def merge_kernel(own_ref, got_ref, *outs):
    y = lax.axis_index("y")
    for s, out_ref in zip(STEPS, outs):
        there = lax.rem(y + s, NY)
        out_ref[...] = (own_ref[there] + got_ref[there].astype(f32)).astype(out_ref.dtype)


def final_kernel(hidden_ref, *refs):
    total = refs[0][...]
    for ref in refs[1:-1]:
        total = total + ref[...].astype(f32)
    refs[-1][...] = (hidden_ref[...].astype(f32) + total).astype(bf16)


def body(
    context,
    residual_in,
    out_weight,
    norm_gain,
    expert_ids,
    gate_weights,
    gate_matrix,
    lift_matrix,
    down_matrix,
):
    tokens, width = residual_in.shape
    top = expert_ids.shape[1]
    share = width // NX
    fine = share // NY
    units = gate_matrix.shape[2]
    capacity = min(tokens, max(2, tokens * top * 9 // (8 * NE)))
    blocks = NY * NC
    slots = blocks * capacity
    contexts = [shift(context, "y", NY, s) for s in STEPS]
    weight = jnp.concatenate(z_ring(out_weight.T), axis=0)
    packed = call(
        route_kernel,
        "route",
        [shape(tokens + TABLE, fine)] * NY,
        expert_ids.T,
        gate_weights.T,
        residual_in,
    )
    down_here, weight = lax.optimization_barrier((down_matrix[0], weight))
    downs = call(cut_kernel, "cut", [shape(units, share)] * NX, down_here)
    gain = norm_gain.astype(f32).reshape(NX, share)
    gain, contexts[0] = lax.optimization_barrier((gain, contexts[0]))
    weight, contexts = lax.optimization_barrier((weight, contexts))
    parts = call(
        project_kernel,
        "project",
        [shape(NY, tokens, fine, dtype=f32)] + [shape(NY, tokens, fine)] * (NX - 1),
        *contexts,
        weight,
        swap(weight),
        scratch=[pltpu.VMEM((NZ, NC * weight.shape[0] // NZ, share), bf16)],
        flops=2 * NY * tokens * share * width // NY,
    )
    parts, packed = lax.optimization_barrier((parts, packed))
    parts = x_exchange(parts)
    packed = y_exchange(packed)
    table = swap(call(pick_kernel, "pick", shape(NY, TABLE, tokens), *packed))
    parts, table, downs = lax.optimization_barrier((parts, table, downs))
    downs = x_exchange(downs)
    hidden = call(hidden_kernel, "hidden", shape(NY * tokens, fine), *parts, *packed)
    pieces = [shift(hidden, "y", NY, s) for s in STEPS]
    pieces, downs[1:3] = lax.optimization_barrier((pieces, downs[1:3]))
    hidden = call(gather_kernel, "gather", shape(NY * tokens, share), *pieces)
    *sent, own, table = call(
        functools.partial(dispatch_kernel, capacity),
        "dispatch",
        [shape(slots, share)] * NZ
        + [shape(tokens, share), shape(blocks, TABLE, tokens, dtype=f32)],
        *packed,
        table,
        hidden,
        swap(hidden),
        scratch=[pltpu.VMEM((blocks, TABLE, tokens), f32)],
        flops=2 * NZ * slots * blocks * tokens * share,
    )

    gate_here = gate_matrix.reshape(NX, share, units)
    lift_here = lift_matrix.reshape(NX, share, units)

    sent = dict(zip(SHIFTS, sent))
    got, rings, acts = [], [], []
    for i, group in enumerate(GROUPS):
        rows = [sent[s] for s in group]
        if i == 1:
            *rows, got[0] = lax.optimization_barrier((*rows, got[0]))
        elif i > 1:
            at, right, left, far = rings[i - 2]
            *rows, right, left = lax.optimization_barrier((*rows, right, left))
            rings[i - 2] = at, right, left, far
        rows = [shift(r, "z", NZ, s) for r, s in zip(rows, group)]
        if i > 1:
            at, right, left, far = rings[i - 2]
            *rows, far = lax.optimization_barrier((*rows, far))
            rings[i - 2] = at, right, left, far
        if i == 1:
            *rows, downs[3] = lax.optimization_barrier((*rows, downs[3]))
        count = len(group) * slots
        got.append(rows[0] if len(rows) == 1 else call(join_kernel, f"join{i}", shape(count, share), *rows, mib=8))
        if i > 0:
            rings.append(x_ring(got[i - 1], i - 1 in (0, 3)))
    rings.append(x_ring(got[-1], True))
    for i, ring in enumerate(rings):
        count = ring[0].shape[0]
        acts.append(
            call(
                functools.partial(up_kernel, width),
                f"up{i}",
                shape(count, units),
                *ring,
                gain,
                gate_here,
                lift_here,
                flops=4 * count * width * units,
            )
        )
    total = None
    for i, group in enumerate(GROUPS):
        count = got[i].shape[0]
        back = call(
            down_kernel,
            f"down{i}",
            [shape(slots, share)] * len(group),
            *x_ring(acts[i], i in (0, 3)),
            *downs,
            flops=2 * count * NX * units * share,
            grid=(share // 256,),
            specs=(
                [pl.BlockSpec((count, units), lambda i: (0, 0))] * NX
                + [pl.BlockSpec((units, 256), lambda i: (0, i))] * NX,
                [pl.BlockSpec((slots, 256), lambda i: (0, i))] * len(group),
            ),
        )
        lists = [shift(r, "z", NZ, -s) for r, s in zip(back, group)]

        def combine(start, number, dtype, total=total, lists=lists, group=group, i=i):
            part = pl.BlockSpec((1, tokens, share), lambda b: (b, 0, 0))
            there = pl.BlockSpec((1, tokens, share), lambda b: (b + start, 0, 0))
            return call(
                functools.partial(combine_kernel, capacity, start, group),
                f"combine{i}_{start}",
                shape(number, tokens, share, dtype=dtype),
                table,
                *lists,
                *([] if total is None else [total]),
                flops=4 * len(group) * number * 32 * tokens * share,
                grid=(number,),
                specs=(
                    [pl.BlockSpec((1, TABLE, tokens), lambda b: (b + start, 0, 0))]
                    + [pl.BlockSpec((slots, share), lambda b: (0, 0))] * len(group)
                    + ([] if total is None else [there]),
                    part,
                ),
            )

        if i < len(GROUPS) - 1:
            total = combine(0, blocks, f32)
    crossing = combine(NY, NY, bf16)
    mine = combine(0, NY, f32)
    merged = call(
        merge_kernel,
        "merge",
        [shape(tokens, share, dtype=f32)] + [shape(tokens, share)] * (NY - 1),
        mine,
        swap(crossing),
    )
    return call(final_kernel, "final", shape(tokens, share), own, *y_exchange(merged))


def solution(mesh):
    fine = Mesh(mesh.devices.reshape(NZ, NY, NC, NX), ("z", "y", "c", "x"))
    e = ("z", "y", "c")
    placed = (
        P(e, "x"),
        P(e, None),
        P("x", e),
        P(),
        P(e, None),
        P(e, None),
        P(e, None, "x"),
        P(e, None, "x"),
        P(e, "x", None),
    )
    return jax.shard_map(body, mesh=fine, in_specs=placed, out_specs=P(e, "x"), check_vma=False)
```
